512 devices in a mesh: group: 8 (over z), ray: 64 (over y, x, core).
Axes of the slice: x: 4, y: 8, z: 8, core: 2. Of those that a mesh axis runs over, the one named last changes fastest.
Arguments:
- bricks: bfloat16 [16384, 4096], P(('group', 'ray')), may hold values from -6 to 6
- work_bricks: int32 [8, 128], P('group', 'ray'), may hold values from 0 to 16383, as said below
- interp: bfloat16 [32768, 5, 512], P(('group', 'ray')), may hold values from 0 to 0.25
- tile_slot: int32 [32768, 5], P(('group', 'ray')), may hold values from 0 to 127, as said below
- spacing: float32 [32768, 40], P(('group', 'ray')), may hold values from 0.02 to 0.3
- targets: float32 [3, 32768], P(None, ('group', 'ray')), may hold values from 0 to 1
- weight_in: bfloat16 [64, 256], replicated, may hold values from -0.75 to 0.75
- weight_mid: bfloat16 [256, 256], replicated, may hold values from -0.375 to 0.375
- weight_out: bfloat16 [256, 4], replicated, may hold values from -0.375 to 0.375
Outputs:
- brick_grad: float32 [16384, 4096], P(('group', 'ray'))
The draws below stay inside these ranges and needn't reach their ends.
Inputs may be any that keep to these rules, and one draw needn't show every extreme that they name: `work_bricks`: slot j of image group g is held by ray index j // 2 of the group, and its brick's owner, the device brick // 32 counted over group then ray, has that same ray index. Among the 2 slots of one device at most 2 name bricks owned in one image group, and on every device exactly 2 do for some group. `tile_slot`: of the 320 tiles of one device, at most 10 name slots held by one device of the group, and on every device some holder is named exactly 10 times.
All inputs are finite; a program needn't handle non-finite values.
Results may differ from the reference program's by a relative error of at most 0.0022.
Values may be sent and summed in bfloat16 or wider, within the bound.
A program may use at most 64 MiB of HBM per device.

```python
import math
import jax
import jax.numpy as jnp
from jax import lax

VOXEL_CHANNELS = 64
BRICK_VOXELS = 64
HID = 256
B_DEV = 32
W_DEV = 2
R_DEV = 64
BRICKS_PER_RAY = 5
BRICK_SAMPLES = 8
NB = 16384
RAY_TOTAL = 32768
N_GROUP = 8
N_RAY = 64


def draw_work_bricks(key, part):
    blocks = N_GROUP * N_RAY
    block_keys = jax.random.split(key, blocks)

    def one_block(block_key, block_index):
        first_key, second_key, third_key = jax.random.split(block_key, 3)
        chosen = jax.random.permutation(first_key, N_GROUP)
        position = jnp.arange(W_DEV)
        pattern = jnp.where(position == 0, 0, (position - 1) % N_GROUP)
        shuffled = jax.random.permutation(second_key, W_DEV)
        owner_group = chosen[pattern[shuffled]]
        local_index = jax.random.randint(third_key, (W_DEV,), 0, B_DEV)
        ray_index = block_index % N_RAY
        return ((owner_group * N_RAY + ray_index) * B_DEV + local_index).astype(jnp.int32)
    rows = jax.vmap(one_block)(block_keys, jnp.arange(blocks))
    return rows.reshape(N_GROUP, N_RAY * W_DEV)


def draw_tile_slot(key, part):
    blocks = N_GROUP * N_RAY
    tiles_each = R_DEV * BRICKS_PER_RAY
    capacity = 2 * tiles_each // N_RAY
    block_keys = jax.random.split(key, blocks)

    def one_block(block_key):
        first_key, second_key, third_key = jax.random.split(block_key, 3)
        chosen = jax.random.permutation(first_key, N_RAY)
        position = jnp.arange(tiles_each)
        pattern = jnp.where(position < capacity, 0, 1 + (position - capacity) % (N_RAY - 1))
        shuffled = jax.random.permutation(second_key, tiles_each)
        holder = chosen[pattern[shuffled]]
        offset = jax.random.randint(third_key, (tiles_each,), 0, W_DEV)
        return (holder * W_DEV + offset).astype(jnp.int32)
    rows = jax.vmap(one_block)(block_keys)
    return rows.reshape(blocks * R_DEV, BRICKS_PER_RAY)


def level_of(rng, dims, shards, smallest, largest):
    gain = 1.0
    for axis_at, shards_of in shards:
        steps = jax.random.uniform(jax.random.fold_in(jax.random.fold_in(rng, 6), axis_at), (shards_of,), jnp.float32, smallest / len(shards), largest / len(shards))
        gain = gain * jnp.repeat(jnp.exp(steps), dims[axis_at] // shards_of).reshape((-1,) + (1,) * (len(dims) - 1 - axis_at))
    return gain


def gaussian(stream_key, dims, spread, bound, cuts=(), kind=jnp.bfloat16):
    drawn = spread * jax.random.normal(stream_key, dims, jnp.float32)
    if cuts:
        drawn = drawn * level_of(stream_key, dims, cuts, -0.22, 0.18)
    return jnp.clip(drawn, -bound, bound).astype(kind)


def setup_inputs(seed: int = 0) -> dict:
    seeds = jax.random.split(jax.random.key(seed), 10)
    bricks = gaussian(seeds[0], (NB, BRICK_VOXELS * VOXEL_CHANNELS), 1.0, 6.0, ((0, 512),))
    work_bricks = draw_work_bricks(jax.random.fold_in(seeds[9], 71), 0)
    interp = jnp.clip(0.25 * jax.random.uniform(seeds[2], (RAY_TOTAL, BRICKS_PER_RAY, BRICK_SAMPLES * BRICK_VOXELS), jnp.float32) ** level_of(seeds[2], (RAY_TOTAL, BRICKS_PER_RAY, BRICK_SAMPLES * BRICK_VOXELS), ((0, 512),), -0.2, 0.2), 0.0, 0.25).astype(jnp.bfloat16)
    tile_slot = draw_tile_slot(jax.random.fold_in(seeds[9], 71), 0)
    spacing = jnp.clip(jnp.exp(math.log(0.3) - 2.7080503 * jax.random.uniform(seeds[4], (RAY_TOTAL, BRICKS_PER_RAY * BRICK_SAMPLES), jnp.float32) ** level_of(seeds[4], (RAY_TOTAL, BRICKS_PER_RAY * BRICK_SAMPLES), ((0, 512),), -0.2, 0.2)), 0.02, 0.3)
    targets = jnp.clip(1.0 * jax.random.uniform(seeds[5], (3, RAY_TOTAL), jnp.float32) ** level_of(seeds[5], (3, RAY_TOTAL), ((1, 512),), -0.2, 0.2), 0.0, 1.0)
    weight_in = gaussian(seeds[6], (VOXEL_CHANNELS, HID), VOXEL_CHANNELS ** -0.5, 0.75)
    weight_mid = gaussian(seeds[7], (HID, HID), HID ** -0.5, 0.375)
    weight_out = gaussian(seeds[8], (HID, 4), HID ** -0.5, 0.375)
    return dict(bricks=bricks, work_bricks=work_bricks, interp=interp, tile_slot=tile_slot, spacing=spacing, targets=targets, weight_in=weight_in, weight_mid=weight_mid, weight_out=weight_out)


def silu_slope(pre_act):
    logistic = jax.nn.sigmoid(pre_act)
    return logistic * (1.0 + pre_act * (1.0 - logistic))

def composite_loss(raw_out, spacing, targets):
    density = jax.nn.softplus(raw_out[:, :, 0])
    shading = jax.nn.sigmoid(raw_out[:, :, 1:4])
    optical = density * spacing
    before_sum = jnp.cumsum(optical, axis=1) - optical
    ray_weight = jnp.exp(-before_sum) * (1.0 - jnp.exp(-optical))
    colour = lax.optimization_barrier(jnp.sum(ray_weight[:, :, None] * shading, axis=1))
    return 0.5 * jnp.sum((colour - targets.T) ** 2)

def feature_grad(features, spacing, targets, weight_in, weight_mid, weight_out):
    pre_first = jnp.dot(features, weight_in, preferred_element_type=jnp.float32)
    act_first = jax.nn.silu(pre_first).astype(jnp.bfloat16)
    pre_second = jnp.dot(act_first, weight_mid, preferred_element_type=jnp.float32)
    act_second = jax.nn.silu(pre_second).astype(jnp.bfloat16)
    raw_out = jnp.dot(act_second, weight_out, preferred_element_type=jnp.float32)
    ray_count = spacing.shape[0]
    raw_grad = jax.grad(composite_loss)(raw_out.reshape(ray_count, -1, 4), spacing, targets)
    raw_grad = raw_grad.reshape(-1, 4).astype(jnp.bfloat16)
    grad_second = jnp.dot(raw_grad, weight_out.T, preferred_element_type=jnp.float32)
    slope_second = (grad_second * silu_slope(pre_second)).astype(jnp.bfloat16)
    grad_first = jnp.dot(slope_second, weight_mid.T, preferred_element_type=jnp.float32)
    slope_first = (grad_first * silu_slope(pre_first)).astype(jnp.bfloat16)
    return jnp.dot(slope_first, weight_in.T, preferred_element_type=jnp.float32).astype(jnp.bfloat16)

def reference(bricks, work_bricks, interp, tile_slot, spacing, targets, weight_in, weight_mid, weight_out):
    count_of_tiles = R_DEV * BRICKS_PER_RAY

    def block_step(accum, block_index):
        group_index = (block_index // N_RAY).astype(jnp.int32)
        first_ray = (block_index * R_DEV).astype(jnp.int32)
        slots = lax.dynamic_slice_in_dim(tile_slot, first_ray, R_DEV, 0).reshape(-1).astype(jnp.int32)
        members = lax.dynamic_index_in_dim(work_bricks, group_index, 0, keepdims=False)
        brick_ids = jnp.take(members, slots, axis=0).astype(jnp.int32)
        tiles = jnp.take(bricks, brick_ids, axis=0).astype(jnp.float32).reshape(count_of_tiles, BRICK_VOXELS, VOXEL_CHANNELS)
        network_weights = lax.dynamic_slice_in_dim(interp, first_ray, R_DEV, 0).astype(jnp.float32)
        network_weights = network_weights.reshape(count_of_tiles, BRICK_SAMPLES, BRICK_VOXELS)
        features = jnp.einsum('tiv,tvc->tic', network_weights, tiles, precision=lax.Precision.HIGHEST)
        features = features.astype(jnp.bfloat16).reshape(-1, VOXEL_CHANNELS)
        ray_space = lax.dynamic_slice_in_dim(spacing, first_ray, R_DEV, 0)
        ray_target = lax.dynamic_slice_in_dim(targets, first_ray, R_DEV, 1)
        tile_gradients = feature_grad(features, ray_space, ray_target, weight_in, weight_mid, weight_out)
        tile_gradients = tile_gradients.astype(jnp.float32).reshape(count_of_tiles, BRICK_SAMPLES, VOXEL_CHANNELS)
        outer = jnp.einsum('tiv,tic->tvc', network_weights, tile_gradients, precision=lax.Precision.HIGHEST)
        return (accum.at[brick_ids].add(outer.reshape(count_of_tiles, BRICK_VOXELS * VOXEL_CHANNELS)), None)
    start = jnp.zeros((NB, BRICK_VOXELS * VOXEL_CHANNELS), jnp.float32)
    total, _ = lax.scan(block_step, start, jnp.arange(N_GROUP * N_RAY, dtype=jnp.int32))
    return total
```

```python
import functools

import jax
import jax.numpy as jnp
from jax import lax
from jax.experimental import pallas as pl
from jax.experimental.pallas import tpu as pltpu
from jax.sharding import PartitionSpec as P

MESH = pl.DeviceIdType.MESH
F32 = jnp.float32
BF16 = jnp.bfloat16
NX = 4
NC = 2
HIGHEST = lax.Precision.HIGHEST


def coordinates():
    ray = lax.axis_index("ray")
    return ray // (NX * NC), (ray // NC) % NX, ray % NC


def ray_of(y, x, c):
    return (y * NX + x) * NC + c


class Peers:
    def __init__(self, nz, ny):
        self.nz, self.ny = nz, ny
        self.z = lax.axis_index("group")
        self.y, self.x, self.c = coordinates()

    def along_z(self, d):
        return {"group": lax.rem(self.z + d, self.nz)}

    def along_y(self, d):
        return {"ray": ray_of(lax.rem(self.y + d, self.ny), self.x, self.c)}

    def along_x(self, d):
        return {"ray": ray_of(self.y, lax.rem(self.x + d, NX), self.c)}

    def partner(self):
        return {"ray": ray_of(self.y, self.x, 1 - self.c)}

    def everybody(self):
        out = [self.along_z(d) for d in range(1, self.nz)]
        out += [self.along_y(d) for d in range(1, self.ny)]
        return out + [self.along_x(1), self.along_x(NX - 1), self.partner()]

    def barrier(self):
        sem = pltpu.get_barrier_semaphore()
        peers = self.everybody()
        for peer in peers:
            pl.semaphore_signal(sem, inc=1, device_id=peer, device_id_type=MESH)
        pl.semaphore_wait(sem, len(peers))


class Copies:
    def __init__(self, send_sems, recv_sems):
        self.send_sems, self.recv_sems, self.count, self.live = send_sems, recv_sems, 0, []

    def make(self, src, dst, device):
        at = self.count
        self.count += 1
        copy = pltpu.make_async_remote_copy(
            src_ref=src,
            dst_ref=dst,
            send_sem=self.send_sems.at[at],
            recv_sem=self.recv_sems.at[at],
            device_id=device,
            device_id_type=MESH,
        )
        self.live.append(copy)
        return copy

    def start(self, src, dst, device):
        copy = self.make(src, dst, device)
        copy.start()
        return copy

    def drain(self):
        for copy in self.live:
            copy.wait_send()


def near_first(n):
    out = []
    for d in range(1, n // 2 + 1):
        out.append(d)
        if n - d != d:
            out.append(n - d)
    return out


def fetch_copies(nz, ny):
    return 2 * (nz - 1) + (ny - 1) + 3 * ny + 4 * ny


def fetch_kernel(
    nz, ny, wb_ref, bricks_ref, gs_ref, reqs_ref, mine, picks, sendb, arrived, send_sems, recv_sems
):
    peers = Peers(nz, ny)
    copies = Copies(send_sems, recv_sems)
    own_count = bricks_ref.shape[0]
    row = lax.broadcasted_iota(jnp.int32, mine.shape, 0)
    tile = jnp.where(row == 0, wb_ref[0, 0], wb_ref[0, 1])
    mine[...] = tile
    reqs_ref[0] = tile
    peers.barrier()
    asks = [
        copies.start(mine, reqs_ref.at[nz - d], peers.along_z(d)) for d in near_first(nz)
    ]
    for ask in asks:
        ask.wait_recv()
    base = (lax.axis_index("group") * lax.axis_size("ray") + lax.axis_index("ray")) * own_count
    lane = lax.broadcasted_iota(jnp.int32, (nz, 128), 1)
    rows = []
    for s in range(2):
        ids = jnp.concatenate([reqs_ref[e, s : s + 1, :] for e in range(nz)], axis=0)
        rows.append(jnp.where(ids - base == lane, 1.0, 0.0).astype(F32))
    choose = jnp.concatenate(rows, axis=0)[:, :own_count].astype(BF16)
    picked = jnp.dot(choose, bricks_ref[...], preferred_element_type=F32)
    for s in range(2):
        for p in range(32):
            picks[pl.ds(s * 32 + p, nz, stride=64), :] = picked[
                s * nz : (s + 1) * nz, p * 128 : (p + 1) * 128
            ]
    sendb[...] = picks[...].reshape(nz, 2, 32, 128).astype(BF16)
    gives = [
        copies.start(sendb.at[d], arrived.at[nz - d], peers.along_z(d)) for d in near_first(nz)
    ]
    held = sendb[0].astype(F32)
    for d, give in zip(near_first(nz), gives):
        give.wait_recv()
        held = held + arrived[nz - d].astype(F32)
    gs_ref[0, 0, 0] = held.astype(BF16)
    spread = {
        ny - d: copies.start(gs_ref.at[0, 0, 0], gs_ref.at[0, 0, ny - d], peers.along_y(d))
        for d in near_first(ny)
    }
    order = [0] + [ny - d for d in near_first(ny)]
    right, left, partner = peers.along_x(1), peers.along_x(NX - 1), peers.partner()
    from_left, from_right, cores = {}, {}, []
    for e in order:
        if e:
            spread[e].wait_recv()
        block = gs_ref.at[0, 0, e]
        from_left[e] = copies.start(block, gs_ref.at[0, 3, e], right)
        from_right[e] = copies.start(block, gs_ref.at[0, 1, e], left)
        cores.append(copies.start(block, gs_ref.at[1, 0, e], partner))
    relays = {}
    for n, e in enumerate(order):
        from_left[e].wait_recv()
        if n % 2 == 0:
            relays[e] = copies.start(gs_ref.at[0, 3, e], gs_ref.at[0, 2, e], right)
        cores.append(copies.start(gs_ref.at[0, 3, e], gs_ref.at[1, 3, e], partner))
        from_right[e].wait_recv()
        if n % 2 == 1:
            relays[e] = copies.start(gs_ref.at[0, 1, e], gs_ref.at[0, 2, e], left)
        cores.append(copies.start(gs_ref.at[0, 1, e], gs_ref.at[1, 1, e], partner))
    for e in order:
        relays[e].wait_recv()
        cores.append(copies.start(gs_ref.at[0, 2, e], gs_ref.at[1, 2, e], partner))
    for copy in cores:
        copy.wait_recv()
    copies.drain()


def fetch(nz, ny, work_bricks, bricks):
    total = fetch_copies(nz, ny)
    vmem = pl.BlockSpec(memory_space=pltpu.VMEM)
    return pl.pallas_call(
        functools.partial(fetch_kernel, nz, ny),
        out_shape=(
            jax.ShapeDtypeStruct((2, NX, ny, 2, 32, 128), BF16),
            jax.ShapeDtypeStruct((nz, 8, 128), jnp.int32),
        ),
        in_specs=[pl.BlockSpec(memory_space=pltpu.SMEM), vmem],
        out_specs=(vmem, vmem),
        scratch_shapes=[
            pltpu.VMEM((8, 128), jnp.int32),
            pltpu.VMEM((nz * 64, 128), F32),
            pltpu.VMEM((nz, 2, 32, 128), BF16),
            pltpu.VMEM((nz, 2, 32, 128), BF16),
            pltpu.SemaphoreType.DMA((total,)),
            pltpu.SemaphoreType.DMA((total,)),
        ],
        compiler_params=pltpu.CompilerParams(collective_id=0, has_side_effects=True),
        name="fetch",
    )(work_bricks, bricks)


def reduce_kernel(
    nz,
    ny,
    acc_ref,
    zout_ref,
    cbuf,
    part,
    relay_a,
    relay_b,
    from_left,
    from_right,
    ybuf,
    send_sems,
    recv_sems,
):
    peers = Peers(nz, ny)
    copies = Copies(send_sems, recv_sems)
    half = ny // 2
    a, b = pl.ds(0, half), pl.ds(half, half)
    right, left, partner = peers.along_x(1), peers.along_x(NX - 1), peers.partner()
    peers.barrier()
    core = {j: copies.start(acc_ref.at[1, j], cbuf.at[j], partner) for j in (2, 1, 3, 0)}

    def merge(j):
        core[j].wait_recv()
        part[j] = acc_ref[0, j] + cbuf[j]

    merge(2)
    far_a = copies.start(part.at[2, a], relay_a, right)
    far_b = copies.start(part.at[2, b], relay_b, left)
    merge(1)
    left_b = copies.start(part.at[1, b], from_left.at[b], right)
    merge(3)
    right_a = copies.start(part.at[3, a], from_right.at[a], left)
    far_a.wait_recv()
    part[1, a] = part[1, a] + relay_a[...]
    left_a = copies.start(part.at[1, a], from_left.at[a], right)
    far_b.wait_recv()
    part[3, b] = part[3, b] + relay_b[...]
    right_b = copies.start(part.at[3, b], from_right.at[b], left)
    merge(0)
    ys = {}
    right_a.wait_recv()
    left_a.wait_recv()
    part[0, a] = part[0, a] + from_left[a] + from_right[a]
    for e in range(1, half):
        ys[e] = copies.start(part.at[0, e], ybuf.at[ny - e], peers.along_y(e))
    left_b.wait_recv()
    right_b.wait_recv()
    part[0, b] = part[0, b] + from_left[b] + from_right[b]
    for e in range(half, ny):
        ys[e] = copies.start(part.at[0, e], ybuf.at[ny - e], peers.along_y(e))
    mine = part[0, 0]
    for e in range(1, ny):
        ys[e].wait_recv()
        mine = mine + ybuf[ny - e]
    zout_ref[0] = mine
    zs = [copies.start(zout_ref.at[0], zout_ref.at[nz - d], peers.along_z(d)) for d in near_first(nz)]
    for copy in zs:
        copy.wait_recv()
    copies.drain()


def reduce_plane(nz, ny, acc):
    total = 4 + 6 + (ny - 1) + (nz - 1)
    vmem = pl.BlockSpec(memory_space=pltpu.VMEM)
    half = (ny // 2, 2, 32, 128)
    whole = (ny, 2, 32, 128)
    return pl.pallas_call(
        functools.partial(reduce_kernel, nz, ny),
        out_shape=jax.ShapeDtypeStruct((nz, 2, 32, 128), F32),
        in_specs=[vmem],
        out_specs=vmem,
        scratch_shapes=[
            pltpu.VMEM((NX,) + whole, F32),
            pltpu.VMEM((NX,) + whole, F32),
            pltpu.VMEM(half, F32),
            pltpu.VMEM(half, F32),
            pltpu.VMEM(whole, F32),
            pltpu.VMEM(whole, F32),
            pltpu.VMEM(whole, F32),
            pltpu.SemaphoreType.DMA((total,)),
            pltpu.SemaphoreType.DMA((total,)),
        ],
        compiler_params=pltpu.CompilerParams(collective_id=1, has_side_effects=True),
        name="reduce_plane",
    )(acc)


def place_kernel(base_ref, reqs_ref, z_ref, out_ref):
    nz = reqs_ref.shape[0]
    own_count = out_ref.shape[0]
    lane = lax.broadcasted_iota(jnp.int32, (2 * nz, 128), 1)
    ids = jnp.concatenate([reqs_ref[e, 0:2, :] for e in range(nz)], axis=0)
    hit = jnp.where(ids - base_ref[0] == lane, 1.0, 0.0).astype(F32)
    spread = jnp.transpose(hit)[:own_count]
    for p in range(32):
        rows = z_ref[pl.ds(p, 2 * nz, stride=32), :]
        out_ref[:, p * 128 : (p + 1) * 128] = jnp.dot(
            spread, rows, precision=HIGHEST, preferred_element_type=F32
        )


def place(own_count, base, reqs, zout):
    vmem = pl.BlockSpec(memory_space=pltpu.VMEM)
    return pl.pallas_call(
        place_kernel,
        out_shape=jax.ShapeDtypeStruct((own_count, 4096), F32),
        in_specs=[pl.BlockSpec(memory_space=pltpu.SMEM), vmem, vmem],
        out_specs=vmem,
        name="place",
    )(base, reqs, zout.reshape(-1, 128))


def logistic(x):
    return 0.5 * jnp.tanh(0.5 * x) + 0.5


def compute_kernel(
    slots_ref,
    interp_ref,
    gs_ref,
    spacing_ref,
    targets_ref,
    win_ref,
    wmid_ref,
    wout_ref,
    acc_ref,
    wc,
    feat_a,
    feat_b,
    slope_a,
    slope_b,
    raw_s,
    grad_s,
    gfeat,
):
    segs, rays, _ = interp_ref.shape
    chunk = rays * 8
    steps = segs * 8
    unroll = 16

    src = lax.broadcasted_iota(jnp.int32, (128, 512), 0)
    dst = lax.broadcasted_iota(jnp.int32, (128, 512), 1)
    voxel = src % 64
    perm = jnp.where(
        (dst // 128 == (src // 64) * 2 + voxel % 2) & (dst % 128 == voxel // 2), 1.0, 0.0
    ).astype(BF16)
    for seg in range(segs):
        for j in range(4):
            moved = jnp.dot(
                interp_ref[seg, :, j * 128 : (j + 1) * 128], perm, preferred_element_type=F32
            )
            for i2 in range(2):
                for h in range(2):
                    blk = i2 * 2 + h
                    wc[pl.ds(seg * rays * 16 + h * 8 + 2 * j + i2, rays, stride=16), :] = moved[
                        :, blk * 128 : (blk + 1) * 128
                    ]
    acc_ref[...] = jnp.zeros_like(acc_ref)

    def tile_weights(tile):
        return wc[pl.ds(pl.multiple_of(tile * 16, 16), 16), :][:, :32].astype(BF16)

    win = win_ref[...]
    wmid = wmid_ref[...]
    wout = jnp.concatenate([wout_ref[...].astype(F32), jnp.zeros((4, 256), F32)], axis=0).astype(BF16)
    win_wide = jnp.concatenate([win.astype(F32), jnp.zeros((64, 256), F32)], axis=0).astype(BF16)

    for seg in range(segs):

        @pl.loop(0, rays // unroll)
        def _(group):
            for u in range(unroll):
                r = group * unroll + u
                brick = gs_ref[slots_ref[seg, r]]
                made = jnp.dot(tile_weights(seg * rays + r), brick, preferred_element_type=F32)
                feat_a[pl.ds(r, 8, stride=rays), :] = made[:8]
                feat_b[pl.ds(r, 8, stride=rays), :] = made[8:]

        rows = pl.ds(seg * chunk, chunk)
        features = (feat_a[...] + pltpu.roll(feat_b[...], 64, 1))[:, :64].astype(BF16)
        pre = jnp.dot(features, win, preferred_element_type=F32)
        s = logistic(pre)
        act = pre * s
        slope_a[rows, :] = s * (1.0 + (pre - act))
        pre = jnp.dot(act.astype(BF16), wmid, preferred_element_type=F32)
        s = logistic(pre)
        act = pre * s
        slope_b[rows, :] = s * (1.0 + (pre - act))
        raw = lax.dot_general(
            wout, act.astype(BF16), (((1,), (1,)), ((), ())), preferred_element_type=F32
        )
        turned = pltpu.roll(raw, chunk - rays, 1)
        for i in range(0, 8, 2):
            at = i * rays
            raw_s[pl.ds(seg * 8 + i, 8, stride=steps), :] = raw[:, at : at + 128]
            raw_s[pl.ds(seg * 8 + i + 1, 8, stride=steps), :] = turned[:, at : at + 128]

    spacing = spacing_ref[...]
    k0 = lax.broadcasted_iota(jnp.int32, (steps, steps), 0)
    k1 = lax.broadcasted_iota(jnp.int32, (steps, steps), 1)
    earlier = jnp.where(k1 < k0, 1.0, 0.0).astype(F32)
    later = jnp.where(k1 > k0, 1.0, 0.0).astype(F32)
    raw0 = raw_s[0:steps, :][:, :rays]
    density = jnp.maximum(raw0, 0.0) + jnp.log1p(jnp.exp(-jnp.abs(raw0)))
    optical = density * spacing
    before = jnp.dot(earlier, optical, precision=HIGHEST, preferred_element_type=F32)
    through = jnp.exp(-before)
    kept = jnp.exp(-optical)
    weight = through * (1.0 - kept)
    pull = jnp.zeros_like(weight)
    grads = []
    for ch in range(3):
        shade = logistic(raw_s[(ch + 1) * steps : (ch + 2) * steps, :][:, :rays])
        colour = jnp.sum(weight * shade, axis=0, keepdims=True)
        err = colour - targets_ref[ch : ch + 1, :]
        pull = pull + err * shade
        grads.append(err * weight * shade * (1.0 - shade))
    after = jnp.dot(later, pull * weight, precision=HIGHEST, preferred_element_type=F32)
    grads.insert(0, (pull * through * kept - after) * spacing * logistic(raw0))
    grad_s[...] = jnp.zeros_like(grad_s)
    for ch in range(4):
        grad_s[ch * steps : (ch + 1) * steps, :rays] = grads[ch]

    for seg in range(segs):
        pieces = []
        for i in range(0, 8, 2):
            even = grad_s[pl.ds(seg * 8 + i, 8, stride=steps), :]
            odd = grad_s[pl.ds(seg * 8 + i + 1, 8, stride=steps), :]
            pieces.append(even + pltpu.roll(odd, rays, 1))
        raw_grad = jnp.concatenate(pieces, axis=1).astype(BF16)
        rows = pl.ds(seg * chunk, chunk)
        grad = lax.dot_general(
            raw_grad, wout, (((0,), (0,)), ((), ())), preferred_element_type=F32
        )
        slope = (grad * slope_b[rows, :]).astype(BF16)
        grad = lax.dot_general(slope, wmid, (((1,), (1,)), ((), ())), preferred_element_type=F32)
        slope = (grad * slope_a[rows, :]).astype(BF16)
        grad = lax.dot_general(
            slope, win_wide, (((1,), (1,)), ((), ())), preferred_element_type=F32
        )
        gfeat[...] = grad.astype(BF16).astype(F32)

        @pl.loop(0, rays // unroll)
        def _(group):
            for u in range(unroll):
                r = group * unroll + u
                g = gfeat[pl.ds(r, 8, stride=rays), :]
                both = jnp.concatenate([g, pltpu.roll(g, 64, 1)], axis=0).astype(BF16)
                outer = lax.dot_general(
                    tile_weights(seg * rays + r),
                    both,
                    (((0,), (0,)), ((), ())),
                    preferred_element_type=F32,
                )
                slot = slots_ref[seg, r]
                acc_ref[slot] = acc_ref[slot] + outer


def compute(slots, interp, gs, spacing, targets, weight_in, weight_mid, weight_out):
    segs, rays, _ = interp.shape
    tiles, samples = segs * rays, segs * rays * 8
    vmem = pl.BlockSpec(memory_space=pltpu.VMEM)
    return pl.pallas_call(
        compute_kernel,
        out_shape=jax.ShapeDtypeStruct(gs.shape, F32),
        in_specs=[pl.BlockSpec(memory_space=pltpu.SMEM)] + [vmem] * 7,
        out_specs=vmem,
        scratch_shapes=[
            pltpu.VMEM((tiles * 16, 128), F32),
            pltpu.VMEM((rays * 8, 128), F32),
            pltpu.VMEM((rays * 8, 128), F32),
            pltpu.VMEM((samples, 256), F32),
            pltpu.VMEM((samples, 256), F32),
            pltpu.VMEM((8 * segs * 8, 128), F32),
            pltpu.VMEM((8 * segs * 8, 128), F32),
            pltpu.VMEM((rays * 8, 128), F32),
        ],
        compiler_params=pltpu.CompilerParams(vmem_limit_bytes=50 * 2**20),
        name="compute",
    )(slots, interp, gs, spacing, targets, weight_in, weight_mid, weight_out)


def per_device(
    bricks, work_bricks, interp, tile_slot, spacing, targets, weight_in, weight_mid, weight_out
):
    nz = lax.axis_size("group")
    ny = lax.axis_size("ray") // (NX * NC)
    y, x, c = coordinates()
    slot = tile_slot.T
    holder = slot // 2
    rel_y = (holder // (NX * NC) - y + ny) % ny
    rel_x = ((holder // NC) % NX - x + NX) % NX
    rel_c = jnp.abs(holder % NC - c)
    slots = ((rel_c * NX + rel_x) * ny + rel_y) * 2 + slot % 2
    own_count = bricks.shape[0]
    base = (lax.axis_index("group") * lax.axis_size("ray") + lax.axis_index("ray")) * own_count
    gs, reqs = fetch(nz, ny, work_bricks, bricks)
    acc = compute(
        slots,
        interp.transpose(1, 0, 2),
        gs.reshape(-1, 32, 128),
        spacing.T,
        targets,
        weight_in,
        weight_mid,
        weight_out.T,
    )
    zout = reduce_plane(nz, ny, acc.reshape(gs.shape))
    return place(own_count, base.reshape(1), reqs, zout)


def solution(mesh):
    in_specs = (
        P(("group", "ray"), None),
        P("group", "ray"),
        P(("group", "ray"), None, None),
        P(("group", "ray"), None),
        P(("group", "ray"), None),
        P(None, ("group", "ray")),
        P(),
        P(),
        P(),
    )
    out_specs = P(("group", "ray"), None)
    return jax.shard_map(
        per_device, mesh=mesh, in_specs=in_specs, out_specs=out_specs, check_vma=False
    )
```

```python
import functools

import jax
import jax.numpy as jnp
from jax import lax
from jax.experimental import pallas as pl
from jax.experimental.pallas import tpu as pltpu
from jax.sharding import PartitionSpec as P

MESH = pl.DeviceIdType.MESH
F32 = jnp.float32
BF16 = jnp.bfloat16
NX = 4
NC = 2
PIECES = 1
PITCH = 40
HIGHEST = lax.Precision.HIGHEST


def coordinates():
    ray = lax.axis_index("ray")
    return ray // (NX * NC), (ray // NC) % NX, ray % NC


def ray_of(y, x, c):
    return (y * NX + x) * NC + c


class Peers:
    def __init__(self, nz, ny):
        self.nz, self.ny = nz, ny
        self.z = lax.axis_index("group")
        self.y, self.x, self.c = coordinates()

    def along_z(self, d):
        return {"group": lax.rem(self.z + d, self.nz)}

    def along_y(self, d):
        return {"ray": ray_of(lax.rem(self.y + d, self.ny), self.x, self.c)}

    def along_x(self, d):
        return {"ray": ray_of(self.y, lax.rem(self.x + d, NX), self.c)}

    def partner(self):
        return {"ray": ray_of(self.y, self.x, 1 - self.c)}

    def everybody(self):
        out = [self.along_z(d) for d in range(1, self.nz)]
        out += [self.along_y(d) for d in range(1, self.ny)]
        return out + [self.along_x(d) for d in range(1, NX)] + [self.partner()]

    def barrier(self):
        sem = pltpu.get_barrier_semaphore()
        peers = self.everybody()
        for peer in peers:
            pl.semaphore_signal(sem, inc=1, device_id=peer, device_id_type=MESH)
        pl.semaphore_wait(sem, len(peers))


class Copies:
    def __init__(self, send_sems, recv_sems):
        self.send_sems, self.recv_sems, self.count, self.live = send_sems, recv_sems, 0, []

    def make(self, src, dst, device):
        at = self.count
        self.count += 1
        copy = pltpu.make_async_remote_copy(
            src_ref=src,
            dst_ref=dst,
            send_sem=self.send_sems.at[at],
            recv_sem=self.recv_sems.at[at],
            device_id=device,
            device_id_type=MESH,
        )
        self.live.append(copy)
        return copy

    def start(self, src, dst, device):
        copy = self.make(src, dst, device)
        copy.start()
        return copy

    def drain(self):
        for copy in self.live:
            copy.wait_send()


def near_first(n):
    out = []
    for d in range(1, n // 2 + 1):
        out.append(d)
        if n - d != d:
            out.append(n - d)
    return out


def fetch_copies(nz, ny):
    return (nz - 1) + 2 * ((nz - 1) + (ny - 1)) + 3 * ny + 4 * ny


def fetch_kernel(
    nz,
    ny,
    wb_ref,
    slot_ref,
    bricks_hbm,
    gs_hbm,
    reqs_ref,
    place_ref,
    mine,
    bricks,
    picks,
    sendb,
    arrived,
    gs,
    load_sem,
    save_sem,
    send_sems,
    recv_sems,
):
    peers = Peers(nz, ny)
    copies = Copies(send_sems, recv_sems)
    load = pltpu.make_async_copy(bricks_hbm, bricks, load_sem.at[0])
    load.start()
    own_count = bricks.shape[0]
    row = lax.broadcasted_iota(jnp.int32, mine.shape, 0)
    tile = jnp.where(row == 0, wb_ref[0, 0], wb_ref[0, 1])
    mine[...] = tile
    reqs_ref[0] = tile
    peers.barrier()
    asks = [copies.start(mine, reqs_ref.at[nz - d], peers.along_z(d)) for d in near_first(nz)]
    slot = slot_ref[...]
    holder = slot // 2
    rel_y = lax.rem(holder // (NX * NC) + (ny - peers.y), ny)
    rel_x = lax.rem(lax.rem(holder // NC, NX) + (NX - peers.x), NX)
    rel_c = jnp.abs(lax.rem(holder, NC) - peers.c)
    place_ref[...] = ((rel_c * NX + rel_x) * ny + rel_y) * 2 + lax.rem(slot, 2)
    load.wait()
    for ask in asks:
        ask.wait_recv()
    base = (lax.axis_index("group") * lax.axis_size("ray") + lax.axis_index("ray")) * own_count
    lane = lax.broadcasted_iota(jnp.int32, (nz, 128), 1)
    rows = []
    for s in range(2):
        ids = jnp.concatenate([reqs_ref[e, s : s + 1, :] for e in range(nz)], axis=0)
        rows.append(jnp.where(ids - base == lane, 1.0, 0.0).astype(F32))
    choose = jnp.concatenate(rows, axis=0)[:, :own_count].astype(BF16)
    picked = jnp.dot(choose, bricks[...], preferred_element_type=F32)
    gives = {}
    for s in range(2):
        for p in range(32):
            picks[pl.ds(s * nz * PITCH + p, nz, stride=PITCH), :] = picked[
                s * nz : (s + 1) * nz, p * 128 : (p + 1) * 128
            ]
        rows = picks[s * nz * PITCH : (s + 1) * nz * PITCH, :].reshape(nz, PITCH, 128)
        sendb[s] = rows[:, :32].astype(BF16)
        for d in near_first(nz):
            gives[s, d] = copies.start(
                sendb.at[s, d], arrived.at[s, nz - d], peers.along_z(d)
            )
    right, far, left = (peers.along_x(d) for d in (1, 2, 3))
    partner = peers.partner()
    order = [0] + [ny - d for d in near_first(ny)]
    spread, hops, cores = {}, {}, []

    def to_core(j, e):
        cores.append(copies.start(gs.at[j, e], gs_hbm.at[1, j, e], partner))

    def along_row(e):
        for j, device in ((3, right), (1, left), (2, far)):
            hops[j, e] = copies.start(gs.at[0, e], gs.at[j, e], device)
        to_core(0, e)

    for s in range(2):
        held = sendb[s, 0].astype(F32)
        for d in near_first(nz):
            gives[s, d].wait_recv()
            held = held + arrived[s, nz - d].astype(F32)
        gs[0, 0, s] = held.astype(BF16)
        for d in near_first(ny):
            spread[s, ny - d] = copies.start(
                gs.at[0, 0, s], gs.at[0, ny - d, s], peers.along_y(d)
            )
    along_row(0)
    for e in order[1:]:
        spread[0, e].wait_recv()
        spread[1, e].wait_recv()
        along_row(e)
    for e in order:
        for j in (3, 1, 2):
            hops[j, e].wait_recv()
            to_core(j, e)
    save = pltpu.make_async_copy(gs, gs_hbm.at[0], save_sem.at[0])
    save.start()
    for copy in cores:
        copy.wait_recv()
    save.wait()
    copies.drain()


def fetch(nz, ny, work_bricks, slots, bricks):
    total = fetch_copies(nz, ny)
    vmem = pl.BlockSpec(memory_space=pltpu.VMEM)
    hbm = pl.BlockSpec(memory_space=pltpu.HBM)
    return pl.pallas_call(
        functools.partial(fetch_kernel, nz, ny),
        out_shape=(
            jax.ShapeDtypeStruct((NC, NX, ny, 2, 32, 128), BF16),
            jax.ShapeDtypeStruct((nz, 8, 128), jnp.int32),
            jax.ShapeDtypeStruct(slots.shape, jnp.int32),
        ),
        in_specs=[pl.BlockSpec(memory_space=pltpu.SMEM), vmem, hbm],
        out_specs=(hbm, vmem, vmem),
        scratch_shapes=[
            pltpu.VMEM((8, 128), jnp.int32),
            pltpu.VMEM(bricks.shape, BF16),
            pltpu.VMEM((2 * nz * PITCH, 128), F32),
            pltpu.VMEM((2, nz, 32, 128), BF16),
            pltpu.VMEM((2, nz, 32, 128), BF16),
            pltpu.VMEM((NX, ny, 2, 32, 128), BF16),
            pltpu.SemaphoreType.DMA((1,)),
            pltpu.SemaphoreType.DMA((1,)),
            pltpu.SemaphoreType.DMA((total,)),
            pltpu.SemaphoreType.DMA((total,)),
        ],
        compiler_params=pltpu.CompilerParams(collective_id=0, has_side_effects=True),
        name="fetch",
    )(work_bricks, slots, bricks)


def reduce_kernel(
    nz,
    ny,
    acc_hbm,
    zout_ref,
    cbuf,
    part,
    relay_a,
    relay_b,
    from_left,
    from_right,
    ybuf,
    load_sems,
    send_sems,
    recv_sems,
):
    peers = Peers(nz, ny)
    copies = Copies(send_sems, recv_sems)
    slices = acc_hbm.shape[0]
    used = pl.ds(0, acc_hbm.shape[-2])
    half = ny // 2
    a, b = pl.ds(0, half), pl.ds(half, half)
    right, left, partner = peers.along_x(1), peers.along_x(NX - 1), peers.partner()
    loads = []
    for q in range(slices):
        load = pltpu.make_async_copy(acc_hbm.at[q, 0], part.at[q], load_sems.at[q])
        load.start()
        loads.append(load)
    peers.barrier()
    core, far_a, far_b, left_a, left_b, right_a, right_b = {}, {}, {}, {}, {}, {}, {}
    for q in range(slices):
        for j in (2, 1, 3, 0):
            core[q, j] = copies.start(acc_hbm.at[q, 1, j], cbuf.at[q, j], partner)

    def merge(q, j):
        core[q, j].wait_recv()
        part[q, j] = part[q, j] + cbuf[q, j]

    for q in range(slices):
        loads[q].wait()
        merge(q, 2)
        far_a[q] = copies.start(part.at[q, 2, a], relay_a.at[q], right)
        far_b[q] = copies.start(part.at[q, 2, b], relay_b.at[q], left)
        merge(q, 1)
        left_b[q] = copies.start(part.at[q, 1, b], from_left.at[q, b], right)
        merge(q, 3)
        right_a[q] = copies.start(part.at[q, 3, a], from_right.at[q, a], left)
    for q in range(slices):
        far_a[q].wait_recv()
        part[q, 1, a] = part[q, 1, a] + relay_a[q]
        left_a[q] = copies.start(part.at[q, 1, a], from_left.at[q, a], right)
        far_b[q].wait_recv()
        part[q, 3, b] = part[q, 3, b] + relay_b[q]
        right_b[q] = copies.start(part.at[q, 3, b], from_right.at[q, b], left)
        merge(q, 0)
    ys, zs = {}, []
    for q in range(slices):
        for copy, side in ((right_a, a), (left_a, a), (left_b, b), (right_b, b)):
            copy[q].wait_recv()
        part[q, 0] = part[q, 0] + from_left[q] + from_right[q]
        for d in near_first(ny):
            ys[q, d] = copies.start(part.at[q, 0, d], ybuf.at[q, ny - d], peers.along_y(d))
    for q in range(slices):
        mine = part[q, 0, 0]
        for d in near_first(ny):
            ys[q, d].wait_recv()
            mine = mine + ybuf[q, ny - d]
        zout_ref[q, 0, used] = mine
        for d in near_first(nz):
            zs.append(
                copies.start(
                    zout_ref.at[q, 0, used], zout_ref.at[q, nz - d, used], peers.along_z(d)
                )
            )
    for copy in zs:
        copy.wait_recv()
    copies.drain()


def reduce_plane(nz, ny, acc):
    slices, unit = acc.shape[0], acc.shape[-2:]
    total = slices * (4 + 6 + (ny - 1) + (nz - 1))
    vmem = pl.BlockSpec(memory_space=pltpu.VMEM)
    half = (slices, ny // 2) + unit
    whole = (slices, ny) + unit
    every = (slices, NX, ny) + unit
    return pl.pallas_call(
        functools.partial(reduce_kernel, nz, ny),
        out_shape=jax.ShapeDtypeStruct((slices, nz, unit[0] + 8, 128), F32),
        in_specs=[pl.BlockSpec(memory_space=pltpu.HBM)],
        out_specs=vmem,
        scratch_shapes=[
            pltpu.VMEM(every, F32),
            pltpu.VMEM(every, F32),
            pltpu.VMEM(half, F32),
            pltpu.VMEM(half, F32),
            pltpu.VMEM(whole, F32),
            pltpu.VMEM(whole, F32),
            pltpu.VMEM(whole, F32),
            pltpu.SemaphoreType.DMA((slices,)),
            pltpu.SemaphoreType.DMA((total,)),
            pltpu.SemaphoreType.DMA((total,)),
        ],
        compiler_params=pltpu.CompilerParams(collective_id=1, has_side_effects=True),
        name="reduce_plane",
    )(acc)


def place_kernel(unit, base_ref, reqs_ref, z_ref, out_ref):
    nz = reqs_ref.shape[0]
    own_count = out_ref.shape[0]
    lane = lax.broadcasted_iota(jnp.int32, (2 * nz, 128), 1)
    ids = [reqs_ref[e, s : s + 1, :] for s in range(2) for e in range(nz)]
    hit = jnp.where(jnp.concatenate(ids, axis=0) - base_ref[0] == lane, 1.0, 0.0).astype(F32)
    spread = jnp.transpose(hit)[:own_count]
    for p in range(32):
        at = p // unit * (2 * nz * (unit + 8)) + p % unit
        rows = z_ref[pl.ds(at, 2 * nz, stride=unit + 8), :]
        out_ref[:, p * 128 : (p + 1) * 128] = jnp.dot(
            spread, rows, precision=HIGHEST, preferred_element_type=F32
        )


def place(own_count, base, reqs, zout):
    vmem = pl.BlockSpec(memory_space=pltpu.VMEM)
    return pl.pallas_call(
        functools.partial(place_kernel, zout.shape[-2] - 8),
        out_shape=jax.ShapeDtypeStruct((own_count, 4096), F32),
        in_specs=[pl.BlockSpec(memory_space=pltpu.SMEM), vmem, vmem],
        out_specs=vmem,
        name="place",
    )(base, reqs, zout.reshape(-1, 128))


def logistic(x):
    return 0.5 * jnp.tanh(0.5 * x) + 0.5


def silu_of_half(half):
    t = jnp.tanh(half)
    up = 1.0 + t
    act = half * up
    return act, up + act * (1.0 - t)


def compute_kernel(
    slots_ref,
    interp_hbm,
    gs_hbm,
    win_hbm,
    wmid_hbm,
    wout_hbm,
    spacing_hbm,
    targets_hbm,
    acc_hbm,
    interp_ref,
    gs_ref,
    win_ref,
    wmid_ref,
    wout_ref,
    spacing_ref,
    targets_ref,
    acc_ref,
    load_sems,
    wc,
    feat_a,
    feat_b,
    slope_a,
    slope_b,
    raw_s,
    grad_s,
    gfeat,
):
    segs, rays, _ = interp_ref.shape
    chunk = rays * 8
    steps = segs * 8
    pitch = rays + 8
    unroll = 16
    pieces_of, unit = acc_ref.shape[0], acc_ref.shape[2]
    loads = []
    for n, (src, dst) in enumerate(
        (
            (interp_hbm, interp_ref),
            (gs_hbm, gs_ref),
            (win_hbm, win_ref),
            (wmid_hbm, wmid_ref),
            (wout_hbm, wout_ref),
            (spacing_hbm, spacing_ref),
            (targets_hbm, targets_ref),
        )
    ):
        loads.append(pltpu.make_async_copy(src, dst, load_sems.at[n]))
        loads[n].start()
    acc_ref[...] = jnp.zeros_like(acc_ref)
    loads[0].wait()

    src = lax.broadcasted_iota(jnp.int32, (128, 512), 0)
    dst = lax.broadcasted_iota(jnp.int32, (128, 512), 1)
    voxel = src % 64
    perm = jnp.where(
        (dst // 128 == (src // 64) * 2 + voxel % 2) & (dst % 128 == voxel // 2), 1.0, 0.0
    ).astype(BF16)
    for seg in range(segs):
        for j in range(4):
            moved = jnp.dot(
                interp_ref[seg, :, j * 128 : (j + 1) * 128], perm, preferred_element_type=F32
            )
            for i2 in range(2):
                for h in range(2):
                    blk = i2 * 2 + h
                    wc[pl.ds(seg * rays * 24 + h * 8 + 2 * j + i2, rays, stride=24), :] = moved[
                        :, blk * 128 : (blk + 1) * 128
                    ]
    for load in loads[1:]:
        load.wait()

    def tile_weights(tile):
        return wc[pl.ds(pl.multiple_of(tile * 24, 8), 16), :][:, :32].astype(BF16)

    win = win_ref[...] * 0.5
    wmid = wmid_ref[...] * 0.5
    wout = jnp.concatenate([wout_ref[...].astype(F32), jnp.zeros((4, 256), F32)], axis=0).astype(BF16)
    win_wide = jnp.concatenate([win.astype(F32), jnp.zeros((64, 256), F32)], axis=0).astype(BF16)

    for seg in range(segs):

        @pl.loop(0, rays // unroll)
        def _(group):
            for u in range(unroll):
                r = group * unroll + u
                brick = gs_ref[slots_ref[seg, r]]
                made = jnp.dot(tile_weights(seg * rays + r), brick, preferred_element_type=F32)
                feat_a[pl.ds(r, 8, stride=pitch), :] = made[:8]
                feat_b[pl.ds(r, 8, stride=pitch), :] = made[8:]

        rows = pl.ds(seg * chunk, chunk)
        features = (feat_a[...] + pltpu.roll(feat_b[...], 64, 1)).reshape(8, pitch, 128)
        features = features[:, :rays].reshape(chunk, 128)[:, :64].astype(BF16)
        act, slope_a[rows, :] = silu_of_half(jnp.dot(features, win, preferred_element_type=F32))
        act, slope_b[rows, :] = silu_of_half(
            jnp.dot(act.astype(BF16), wmid, preferred_element_type=F32)
        )
        raw = lax.dot_general(
            wout, act.astype(BF16), (((1,), (1,)), ((), ())), preferred_element_type=F32
        )
        turned = pltpu.roll(raw, chunk - rays, 1)
        for i in range(0, 8, 2):
            at = i * rays
            raw_s[pl.ds(seg * 8 + i, 8, stride=steps), :] = raw[:, at : at + 128]
            raw_s[pl.ds(seg * 8 + i + 1, 8, stride=steps), :] = turned[:, at : at + 128]

    spacing = spacing_ref[...]
    k0 = lax.broadcasted_iota(jnp.int32, (steps, steps), 0)
    k1 = lax.broadcasted_iota(jnp.int32, (steps, steps), 1)
    earlier = jnp.where(k1 < k0, 1.0, 0.0).astype(F32)
    later = jnp.where(k1 > k0, 1.0, 0.0).astype(F32)
    raw0 = raw_s[0:steps, :][:, :rays]
    density = jnp.maximum(raw0, 0.0) + jnp.log1p(jnp.exp(-jnp.abs(raw0)))
    optical = density * spacing
    before = jnp.dot(earlier, optical, precision=HIGHEST, preferred_element_type=F32)
    through = jnp.exp(-before)
    kept = jnp.exp(-optical)
    weight = through * (1.0 - kept)
    pull = jnp.zeros_like(weight)
    grads = []
    for ch in range(3):
        shade = logistic(raw_s[(ch + 1) * steps : (ch + 2) * steps, :][:, :rays])
        colour = jnp.sum(weight * shade, axis=0, keepdims=True)
        err = colour - targets_ref[ch : ch + 1, :]
        pull = pull + err * shade
        grads.append(err * weight * shade * (1.0 - shade))
    after = jnp.dot(later, pull * weight, precision=HIGHEST, preferred_element_type=F32)
    grads.insert(0, (pull * through * kept - after) * spacing * logistic(raw0))
    grad_s[...] = jnp.zeros_like(grad_s)
    for ch in range(4):
        grad_s[ch * steps : (ch + 1) * steps, :rays] = grads[ch]

    for seg in range(segs):
        pieces = []
        for i in range(0, 8, 2):
            even = grad_s[pl.ds(seg * 8 + i, 8, stride=steps), :]
            odd = grad_s[pl.ds(seg * 8 + i + 1, 8, stride=steps), :]
            pieces.append(even + pltpu.roll(odd, rays, 1))
        raw_grad = jnp.concatenate(pieces, axis=1).astype(BF16)
        rows = pl.ds(seg * chunk, chunk)
        grad = lax.dot_general(
            raw_grad, wout, (((0,), (0,)), ((), ())), preferred_element_type=F32
        )
        slope = (grad * slope_b[rows, :]).astype(BF16)
        grad = lax.dot_general(slope, wmid, (((1,), (1,)), ((), ())), preferred_element_type=F32)
        slope = (grad * slope_a[rows, :]).astype(BF16)
        grad = lax.dot_general(
            slope, win_wide, (((1,), (1,)), ((), ())), preferred_element_type=F32
        )
        grad = grad.astype(BF16).astype(F32)
        for i in range(8):
            gfeat[i * pitch : i * pitch + rays, :] = grad[i * rays : (i + 1) * rays]

        @pl.loop(0, rays // unroll)
        def _(group):
            for u in range(unroll):
                r = group * unroll + u
                g = gfeat[pl.ds(r, 8, stride=pitch), :]
                both = jnp.concatenate([g, pltpu.roll(g, 64, 1)], axis=0).astype(BF16)
                outer = lax.dot_general(
                    tile_weights(seg * rays + r),
                    both,
                    (((0,), (0,)), ((), ())),
                    preferred_element_type=F32,
                )
                slot = slots_ref[seg, r]
                slot = (slot & 1) * (acc_ref.shape[1] // 2) + (slot >> 1)
                for n in range(pieces_of):
                    acc_ref[n, slot] = acc_ref[n, slot] + outer[n * unit : (n + 1) * unit]

    save = pltpu.make_async_copy(acc_ref, acc_hbm, load_sems.at[0])
    save.start()
    save.wait()


def compute(slots, interp, gs, weight_in, weight_mid, weight_out, spacing, targets):
    segs, rays, _ = interp.shape
    tiles, samples = segs * rays, segs * rays * 8
    hbm = pl.BlockSpec(memory_space=pltpu.HBM)
    operands = (interp, gs, weight_in, weight_mid, weight_out, spacing, targets)
    acc = jax.ShapeDtypeStruct((PIECES, gs.shape[0], 32 // PIECES, 128), F32)
    return pl.pallas_call(
        compute_kernel,
        out_shape=acc,
        in_specs=[pl.BlockSpec(memory_space=pltpu.SMEM)] + [hbm] * 7,
        out_specs=hbm,
        scratch_shapes=[pltpu.VMEM(x.shape, x.dtype) for x in operands]
        + [
            pltpu.VMEM(acc.shape, F32),
            pltpu.SemaphoreType.DMA((7,)),
            pltpu.VMEM((tiles * 24, 128), F32),
            pltpu.VMEM(((rays + 8) * 8, 128), F32),
            pltpu.VMEM(((rays + 8) * 8, 128), F32),
            pltpu.VMEM((samples, 256), F32),
            pltpu.VMEM((samples, 256), F32),
            pltpu.VMEM((8 * segs * 8, 128), F32),
            pltpu.VMEM((8 * segs * 8, 128), F32),
            pltpu.VMEM(((rays + 8) * 8, 128), F32),
        ],
        name="compute",
    )(slots, *operands)


def per_device(
    bricks, work_bricks, interp, tile_slot, spacing, targets, weight_in, weight_mid, weight_out
):
    nz = lax.axis_size("group")
    ny = lax.axis_size("ray") // (NX * NC)
    own_count = bricks.shape[0]
    base = (lax.axis_index("group") * lax.axis_size("ray") + lax.axis_index("ray")) * own_count
    gs, reqs, slots = fetch(nz, ny, work_bricks, tile_slot.T, bricks)
    acc = compute(
        slots,
        interp.transpose(1, 0, 2),
        gs.reshape(-1, 32, 128),
        weight_in,
        weight_mid,
        weight_out.T,
        spacing.T,
        targets,
    )
    zout = reduce_plane(nz, ny, acc.reshape((2 * PIECES, NC, NX, ny) + acc.shape[2:]))
    return place(own_count, base.reshape(1), reqs, zout)


def solution(mesh):
    in_specs = (
        P(("group", "ray"), None),
        P("group", "ray"),
        P(("group", "ray"), None, None),
        P(("group", "ray"), None),
        P(("group", "ray"), None),
        P(None, ("group", "ray")),
        P(),
        P(),
        P(),
    )
    out_specs = P(("group", "ray"), None)
    return jax.shard_map(
        per_device, mesh=mesh, in_specs=in_specs, out_specs=out_specs, check_vma=False
    )
```

```python
import functools

import jax
import jax.numpy as jnp
from jax import lax
from jax.experimental import pallas as pl
from jax.experimental.pallas import tpu as pltpu
from jax.sharding import PartitionSpec as P

MESH = pl.DeviceIdType.MESH
F32 = jnp.float32
BF16 = jnp.bfloat16
NX = 4
NC = 2
PITCH = 40
HIGHEST = lax.Precision.HIGHEST


def coordinates():
    ray = lax.axis_index("ray")
    return ray // (NX * NC), (ray // NC) % NX, ray % NC


def ray_of(y, x, c):
    return (y * NX + x) * NC + c


class Peers:
    def __init__(self, nz, ny):
        self.nz, self.ny = nz, ny
        self.z = lax.axis_index("group")
        self.y, self.x, self.c = coordinates()

    def along_z(self, d):
        return {"group": lax.rem(self.z + d, self.nz)}

    def along_y(self, d):
        return {"ray": ray_of(lax.rem(self.y + d, self.ny), self.x, self.c)}

    def along_x(self, d):
        return {"ray": ray_of(self.y, lax.rem(self.x + d, NX), self.c)}

    def partner(self):
        return {"ray": ray_of(self.y, self.x, 1 - self.c)}

    def everybody(self):
        out = [self.along_z(d) for d in range(1, self.nz)]
        out += [self.along_y(d) for d in range(1, self.ny)]
        return out + [self.along_x(d) for d in range(1, NX)] + [self.partner()]

    def greet(self):
        sem = pltpu.get_barrier_semaphore()
        peers = self.everybody()
        for peer in peers:
            pl.semaphore_signal(sem, inc=1, device_id=peer, device_id_type=MESH)
        return lambda: pl.semaphore_wait(sem, len(peers))


class Copies:
    def __init__(self, send_sems, recv_sems):
        self.send_sems, self.recv_sems, self.count, self.live = send_sems, recv_sems, 0, []

    def make(self, src, dst, device):
        at = self.count
        self.count += 1
        copy = pltpu.make_async_remote_copy(
            src_ref=src,
            dst_ref=dst,
            send_sem=self.send_sems.at[at],
            recv_sem=self.recv_sems.at[at],
            device_id=device,
            device_id_type=MESH,
        )
        self.live.append(copy)
        return copy

    def start(self, src, dst, device):
        copy = self.make(src, dst, device)
        copy.start()
        return copy

    def drain(self):
        for copy in self.live:
            copy.wait_send()


def near_first(n):
    out = []
    for d in range(1, n // 2 + 1):
        out.append(d)
        if n - d != d:
            out.append(n - d)
    return out


def logistic(x):
    return 0.5 * jnp.tanh(0.5 * x) + 0.5


def silu_of_half(half):
    t = jnp.tanh(half)
    up = 1.0 + t
    act = half * up
    return act, up + act * (1.0 - t)


def iota(shape, axis):
    return lax.broadcasted_iota(jnp.int32, shape, axis)


def indicator(condition, dtype=F32):
    return jnp.where(condition, 1.0, 0.0).astype(dtype)


def step_copies(nz, ny):
    fetched = 2 * (nz - 1) + (nz - 1) + 2 * (ny - 1) + 3 * ny + 4 * ny
    return fetched + 2 * (4 + 6 + (ny - 1) + (nz - 1))


def step_kernel(
    nz,
    ny,
    wb_ref,
    slots_ref,
    slotv_ref,
    bricks_hbm,
    interp_hbm,
    win_hbm,
    wmid_hbm,
    wout_hbm,
    spacing_hbm,
    targets_hbm,
    zout_ref,
    reqs_ref,
    bricks_ref,
    interp_ref,
    win_ref,
    wmid_ref,
    wout_ref,
    spacing_ref,
    targets_ref,
    mine,
    picks,
    sendb,
    arrived,
    gs,
    wc,
    feat_a,
    feat_b,
    slope_a,
    slope_b,
    raw_s,
    grad_s,
    order_s,
    parity_s,
    wsort,
    wturned,
    gnat,
    gsort,
    outb,
    part,
    cbuf,
    relay_a,
    relay_b,
    from_left,
    from_right,
    ybuf,
    load_sems,
    send_sems,
    recv_sems,
):
    peers = Peers(nz, ny)
    copies = Copies(send_sems, recv_sems)
    segs, rays, _ = interp_ref.shape
    tiles = segs * rays
    holders = NC * NX * ny
    cap = 2 * tiles // holders
    sorted_rows = holders * cap
    chunk = rays * 8
    steps = segs * 8
    pitch = rays + 8
    own_count = bricks_ref.shape[0]
    loads = []
    for n, (src, dst) in enumerate(
        (
            (interp_hbm, interp_ref),
            (bricks_hbm, bricks_ref),
            (win_hbm, win_ref),
            (wmid_hbm, wmid_ref),
            (wout_hbm, wout_ref),
            (spacing_hbm, spacing_ref),
            (targets_hbm, targets_ref),
        )
    ):
        loads.append(pltpu.make_async_copy(src, dst, load_sems.at[n]))
        loads[n].start()
    ask = jnp.where(iota(mine.shape, 0) == 0, wb_ref[0, 0], wb_ref[0, 1])
    mine[...] = ask
    reqs_ref[0] = ask
    barrier = peers.greet()

    slot = slotv_ref[...]
    holder = slot // 2
    rel_y = lax.rem(holder // (NX * NC) + (ny - peers.y), ny)
    rel_x = lax.rem(lax.rem(holder // NC, NX) + (NX - peers.x), NX)
    rel_c = jnp.abs(lax.rem(holder, NC) - peers.c)
    rel = ((rel_c * NX + rel_x) * ny + rel_y).astype(F32)
    parity = lax.rem(slot, 2).astype(F32)

    def as_row(x):
        return jnp.concatenate([x[seg : seg + 1] for seg in range(segs)], axis=1)

    rel, parity = as_row(rel), as_row(parity)
    named = rel == iota((holders, tiles), 0).astype(F32)
    before = indicator(iota((tiles, tiles), 0) < iota((tiles, tiles), 1), BF16)
    counts = jnp.dot(indicator(named, BF16), before, preferred_element_type=F32)
    rank = jnp.sum(jnp.where(named, counts, 0.0), axis=0, keepdims=True)
    taken = rel * cap + rank
    order_s[...] = indicator(iota((sorted_rows, tiles), 0).astype(F32) == taken, BF16)

    src, dst = iota((128, 512), 0), iota((128, 512), 1)
    voxel = src % 64
    perm = indicator(
        (dst // 128 == (src // 64) * 2 + voxel % 2) & (dst % 128 == voxel // 2), BF16
    )
    loads[0].wait()
    for seg in range(segs):
        for j in range(4):
            moved = jnp.dot(
                interp_ref[seg, :, j * 128 : (j + 1) * 128], perm, preferred_element_type=F32
            )
            for i2 in range(2):
                for h in range(2):
                    blk = i2 * 2 + h
                    wc[pl.ds(seg * rays * 24 + h * 8 + 2 * j + i2, rays, stride=24), :] = moved[
                        :, blk * 128 : (blk + 1) * 128
                    ]
    barrier()
    asks = [copies.start(mine, reqs_ref.at[nz - d], peers.along_z(d)) for d in near_first(nz)]

    natural = interp_ref[...].reshape(tiles, 512)
    ordered = jnp.dot(order_s[...], natural, preferred_element_type=F32)
    for j in range(4):
        pair = ordered[:, j * 128 : (j + 1) * 128]
        wsort[pl.ds(2 * j, sorted_rows, stride=8), :] = pair
        wsort[pl.ds(2 * j + 1, sorted_rows, stride=8), :] = pltpu.roll(pair, 64, 1)
    lane128 = iota((sorted_rows, 128), 1)
    wide = jnp.broadcast_to(parity, (128, tiles)).astype(BF16)
    odd = lax.dot_general(
        order_s[...], wide, (((1,), (1,)), ((), ())), preferred_element_type=F32
    )
    parity_s[...] = indicator((lane128 >= 64) == (odd > 0.5))

    def turn(first, last):
        for h in range(first, last):
            block = wsort[h * cap * 8 : (h + 1) * cap * 8, :]
            wturned[h] = jnp.transpose(block)[:64].astype(BF16)

    for load in loads[1:]:
        load.wait()
    for copy in asks:
        copy.wait_recv()
    base = (lax.axis_index("group") * lax.axis_size("ray") + lax.axis_index("ray")) * own_count
    rows = []
    for s in range(2):
        ids = jnp.concatenate([reqs_ref[e, s : s + 1, :] for e in range(nz)], axis=0)
        rows.append(indicator(ids - base == iota((nz, 128), 1)))
    choose = jnp.concatenate(rows, axis=0)[:, :own_count].astype(BF16)
    picked = jnp.dot(choose, bricks_ref[...], preferred_element_type=F32)
    gives = {}
    for s in range(2):
        for p in range(32):
            picks[pl.ds(s * nz * PITCH + p, nz, stride=PITCH), :] = picked[
                s * nz : (s + 1) * nz, p * 128 : (p + 1) * 128
            ]
        rows = picks[s * nz * PITCH : (s + 1) * nz * PITCH, :].reshape(nz, PITCH, 128)
        sendb[s] = rows[:, :32].astype(BF16)
        for d in near_first(nz):
            gives[s, d] = copies.start(sendb.at[s, d], arrived.at[s, nz - d], peers.along_z(d))
    turn(0, holders // 2)
    right, far, left = (peers.along_x(d) for d in (1, 2, 3))
    partner = peers.partner()
    order = [0] + [ny - d for d in near_first(ny)]
    spread, hops, cores = {}, {}, []

    def unit(c, j, e):
        y = lax.rem(peers.y + e, ny)
        x = lax.rem(peers.x + j, NX)
        return ray_of(y, x, c)

    def to_core(j, e):
        at = unit(peers.c, j, e)
        cores.append(copies.start(gs.at[at], gs.at[at], partner))

    def along_row(e):
        at = unit(peers.c, 0, e)
        for j, device in ((3, right), (1, left), (2, far)):
            hops[j, e] = copies.start(gs.at[at], gs.at[at], device)
        to_core(0, e)

    for s in range(2):
        held = sendb[s, 0].astype(F32)
        for d in near_first(nz):
            gives[s, d].wait_recv()
            held = held + arrived[s, nz - d].astype(F32)
        at = unit(peers.c, 0, 0)
        gs[at, s] = held.astype(BF16)
        for d in near_first(ny):
            spread[s, ny - d] = copies.start(gs.at[at, s], gs.at[at, s], peers.along_y(d))
    along_row(0)
    turn(holders // 2, holders)
    for e in order[1:]:
        spread[0, e].wait_recv()
        spread[1, e].wait_recv()
        along_row(e)
    for e in order:
        for j in (3, 1, 2):
            hops[j, e].wait_recv()
            to_core(j, e)
    for copy in cores:
        copy.wait_recv()

    win = win_ref[...] * 0.5
    wmid = wmid_ref[...] * 0.5
    wout = jnp.concatenate([wout_ref[...].astype(F32), jnp.zeros((4, 256), F32)], axis=0).astype(BF16)
    win_wide = jnp.concatenate([win.astype(F32), jnp.zeros((64, 256), F32)], axis=0).astype(BF16)
    unroll = 16
    for seg in range(segs):

        @pl.loop(0, rays // unroll)
        def _(group):
            for u in range(unroll):
                r = group * unroll + u
                name = slots_ref[seg, r]
                brick = gs[name >> 1, name & 1]
                at = pl.multiple_of((seg * rays + r) * 24, 8)
                weights = wc[pl.ds(at, 16), :][:, :32].astype(BF16)
                made = jnp.dot(weights, brick, preferred_element_type=F32)
                feat_a[pl.ds(r, 8, stride=pitch), :] = made[:8]
                feat_b[pl.ds(r, 8, stride=pitch), :] = made[8:]

        rows = pl.ds(seg * chunk, chunk)
        features = (feat_a[...] + pltpu.roll(feat_b[...], 64, 1)).reshape(8, pitch, 128)
        features = features[:, :rays].reshape(chunk, 128)[:, :64].astype(BF16)
        act, slope_a[rows, :] = silu_of_half(jnp.dot(features, win, preferred_element_type=F32))
        act, slope_b[rows, :] = silu_of_half(
            jnp.dot(act.astype(BF16), wmid, preferred_element_type=F32)
        )
        raw = lax.dot_general(
            wout, act.astype(BF16), (((1,), (1,)), ((), ())), preferred_element_type=F32
        )
        turned = pltpu.roll(raw, chunk - rays, 1)
        for i in range(0, 8, 2):
            at = i * rays
            raw_s[pl.ds(seg * 8 + i, 8, stride=steps), :] = raw[:, at : at + 128]
            raw_s[pl.ds(seg * 8 + i + 1, 8, stride=steps), :] = turned[:, at : at + 128]

    spacing = spacing_ref[...]
    k0, k1 = iota((steps, steps), 0), iota((steps, steps), 1)
    earlier, later = indicator(k1 < k0), indicator(k1 > k0)
    raw0 = raw_s[0:steps, :][:, :rays]
    density = jnp.maximum(raw0, 0.0) + jnp.log1p(jnp.exp(-jnp.abs(raw0)))
    optical = density * spacing
    gone = jnp.dot(earlier, optical, precision=HIGHEST, preferred_element_type=F32)
    through = jnp.exp(-gone)
    kept = jnp.exp(-optical)
    weight = through * (1.0 - kept)
    pull = jnp.zeros_like(weight)
    grads = []
    for ch in range(3):
        shade = logistic(raw_s[(ch + 1) * steps : (ch + 2) * steps, :][:, :rays])
        colour = jnp.sum(weight * shade, axis=0, keepdims=True)
        err = colour - targets_ref[ch : ch + 1, :]
        pull = pull + err * shade
        grads.append(err * weight * shade * (1.0 - shade))
    after = jnp.dot(later, pull * weight, precision=HIGHEST, preferred_element_type=F32)
    grads.insert(0, (pull * through * kept - after) * spacing * logistic(raw0))
    grad_s[...] = jnp.zeros_like(grad_s)
    for ch in range(4):
        grad_s[ch * steps : (ch + 1) * steps, :rays] = grads[ch]

    for seg in range(segs):
        pieces = []
        for i in range(0, 8, 2):
            even = grad_s[pl.ds(seg * 8 + i, 8, stride=steps), :]
            uneven = grad_s[pl.ds(seg * 8 + i + 1, 8, stride=steps), :]
            pieces.append(even + pltpu.roll(uneven, rays, 1))
        raw_grad = jnp.concatenate(pieces, axis=1).astype(BF16)
        rows = pl.ds(seg * chunk, chunk)
        grad = lax.dot_general(
            raw_grad, wout, (((0,), (0,)), ((), ())), preferred_element_type=F32
        )
        slope = (grad * slope_b[rows, :]).astype(BF16)
        grad = lax.dot_general(slope, wmid, (((1,), (1,)), ((), ())), preferred_element_type=F32)
        slope = (grad * slope_a[rows, :]).astype(BF16)
        grad = lax.dot_general(
            slope, win_wide, (((1,), (1,)), ((), ())), preferred_element_type=F32
        )
        for j in range(4):
            even = grad[2 * j * rays : (2 * j + 1) * rays]
            uneven = grad[(2 * j + 1) * rays : (2 * j + 2) * rays]
            gnat[seg * rays : (seg + 1) * rays, j * 128 : (j + 1) * 128] = (
                even + pltpu.roll(uneven, 64, 1)
            ).astype(BF16)

    keep = parity_s[...]
    first = lane128 < 64
    for j in range(4):
        pair = jnp.dot(
            order_s[...], gnat[:, j * 128 : (j + 1) * 128], preferred_element_type=F32
        )
        swapped = pltpu.roll(pair, 64, 1)
        gsort[pl.ds(2 * j, sorted_rows, stride=8), :] = jnp.where(first, pair, swapped) * keep
        gsort[pl.ds(2 * j + 1, sorted_rows, stride=8), :] = jnp.where(first, swapped, pair) * keep

    def block(h):
        grads = gsort[h * cap * 8 : (h + 1) * cap * 8, :].astype(BF16)
        return jnp.dot(wturned[h], grads, preferred_element_type=F32)

    half = ny // 2
    a, b = pl.ds(0, half), pl.ds(half, half)
    core, far_a, far_b, left_a, left_b, right_a, right_b = {}, {}, {}, {}, {}, {}, {}
    for j in (2, 1, 3, 0):
        for e in range(ny):
            made = block((NX + j) * ny + e)
            outb[0, j, e] = made[:32]
            outb[1, j, e] = made[32:]
        for q in range(2):
            core[q, j] = copies.start(outb.at[q, j], cbuf.at[q, j], partner)
    for j in (2, 1, 3, 0):
        for e in range(ny):
            made = block(j * ny + e)
            part[0, j, e] = made[:32]
            part[1, j, e] = made[32:]

    def merge(q, j):
        core[q, j].wait_recv()
        part[q, j] = part[q, j] + cbuf[q, j]

    for q in range(2):
        merge(q, 2)
        far_a[q] = copies.start(part.at[q, 2, a], relay_a.at[q], right)
        far_b[q] = copies.start(part.at[q, 2, b], relay_b.at[q], left)
        merge(q, 1)
        left_b[q] = copies.start(part.at[q, 1, b], from_left.at[q, b], right)
        merge(q, 3)
        right_a[q] = copies.start(part.at[q, 3, a], from_right.at[q, a], left)
    for q in range(2):
        far_a[q].wait_recv()
        part[q, 1, a] = part[q, 1, a] + relay_a[q]
        left_a[q] = copies.start(part.at[q, 1, a], from_left.at[q, a], right)
        far_b[q].wait_recv()
        part[q, 3, b] = part[q, 3, b] + relay_b[q]
        right_b[q] = copies.start(part.at[q, 3, b], from_right.at[q, b], left)
        merge(q, 0)
    ys, zs = {}, []
    for q in range(2):
        for copy, side in ((right_a, a), (left_a, a), (left_b, b), (right_b, b)):
            copy[q].wait_recv()
        part[q, 0] = part[q, 0] + from_left[q] + from_right[q]
        for d in near_first(ny):
            ys[q, d] = copies.start(part.at[q, 0, d], ybuf.at[q, ny - d], peers.along_y(d))
    used = pl.ds(0, 32)
    for q in range(2):
        total = part[q, 0, 0]
        for d in near_first(ny):
            ys[q, d].wait_recv()
            total = total + ybuf[q, ny - d]
        zout_ref[q, 0, used] = total
        for d in near_first(nz):
            zs.append(
                copies.start(
                    zout_ref.at[q, 0, used], zout_ref.at[q, nz - d, used], peers.along_z(d)
                )
            )
    for copy in zs:
        copy.wait_recv()
    copies.drain()


def step(nz, ny, work_bricks, slots, *operands):
    bricks, interp = operands[:2]
    segs, rays, _ = interp.shape
    tiles, samples, holders = segs * rays, segs * rays * 8, NC * NX * ny
    cap = 2 * tiles // holders
    total = step_copies(nz, ny)
    vmem = pl.BlockSpec(memory_space=pltpu.VMEM)
    smem = pl.BlockSpec(memory_space=pltpu.SMEM)
    hbm = pl.BlockSpec(memory_space=pltpu.HBM)
    unit = (32, 128)
    every = pltpu.VMEM((2, NX, ny) + unit, F32)
    whole = pltpu.VMEM((2, ny) + unit, F32)
    half = pltpu.VMEM((2, ny // 2) + unit, F32)
    return pl.pallas_call(
        functools.partial(step_kernel, nz, ny),
        out_shape=(
            jax.ShapeDtypeStruct((2, nz, PITCH, 128), F32),
            jax.ShapeDtypeStruct((nz, 8, 128), jnp.int32),
        ),
        in_specs=[smem, smem, vmem] + [hbm] * 7,
        out_specs=(vmem, vmem),
        scratch_shapes=[
            pltpu.VMEM(x.shape, x.dtype)
            for x in (bricks, interp) + operands[2:]
        ]
        + [
            pltpu.VMEM((8, 128), jnp.int32),
            pltpu.VMEM((2 * nz * PITCH, 128), F32),
            pltpu.VMEM((2, nz) + unit, BF16),
            pltpu.VMEM((2, nz) + unit, BF16),
            pltpu.VMEM((holders, 2) + unit, BF16),
            pltpu.VMEM((tiles * 24, 128), F32),
            pltpu.VMEM(((rays + 8) * 8, 128), F32),
            pltpu.VMEM(((rays + 8) * 8, 128), F32),
            pltpu.VMEM((samples, 256), F32),
            pltpu.VMEM((samples, 256), F32),
            pltpu.VMEM((8 * segs * 8, 128), F32),
            pltpu.VMEM((8 * segs * 8, 128), F32),
            pltpu.VMEM((holders * cap, tiles), BF16),
            pltpu.VMEM((holders * cap, 128), F32),
            pltpu.VMEM((holders * cap * 8, 128), F32),
            pltpu.VMEM((holders, 64, cap * 8), BF16),
            pltpu.VMEM((tiles, 512), BF16),
            pltpu.VMEM((holders * cap * 8, 128), F32),
            every,
            every,
            every,
            half,
            half,
            whole,
            whole,
            whole,
            pltpu.SemaphoreType.DMA((7,)),
            pltpu.SemaphoreType.DMA((total,)),
            pltpu.SemaphoreType.DMA((total,)),
        ],
        compiler_params=pltpu.CompilerParams(collective_id=0, has_side_effects=True),
        name="step",
    )(work_bricks, slots, slots, *operands)


def place_kernel(base_ref, reqs_ref, z_ref, out_ref):
    nz = reqs_ref.shape[0]
    own_count = out_ref.shape[0]
    ids = [reqs_ref[e, s : s + 1, :] for s in range(2) for e in range(nz)]
    hit = indicator(jnp.concatenate(ids, axis=0) - base_ref[0] == iota((2 * nz, 128), 1))
    spread = jnp.transpose(hit)[:own_count]
    first = iota((nz, 128), 1) < 64
    for p in range(32):
        at = p // 16 * (nz * PITCH) + p % 16 * 2
        even = z_ref[pl.ds(at, nz, stride=PITCH), :]
        uneven = z_ref[pl.ds(at + 1, nz, stride=PITCH), :]
        rows = jnp.concatenate(
            [
                jnp.where(first, even, pltpu.roll(uneven, 64, 1)),
                jnp.where(first, pltpu.roll(even, 64, 1), uneven),
            ],
            axis=0,
        )
        out_ref[:, p * 128 : (p + 1) * 128] = jnp.dot(
            spread, rows, precision=HIGHEST, preferred_element_type=F32
        )


def place(own_count, base, reqs, zout):
    vmem = pl.BlockSpec(memory_space=pltpu.VMEM)
    return pl.pallas_call(
        place_kernel,
        out_shape=jax.ShapeDtypeStruct((own_count, 4096), F32),
        in_specs=[pl.BlockSpec(memory_space=pltpu.SMEM), vmem, vmem],
        out_specs=vmem,
        name="place",
    )(base, reqs, zout.reshape(-1, 128))


def per_device(
    bricks, work_bricks, interp, tile_slot, spacing, targets, weight_in, weight_mid, weight_out
):
    nz = lax.axis_size("group")
    ny = lax.axis_size("ray") // (NX * NC)
    own_count = bricks.shape[0]
    base = (lax.axis_index("group") * lax.axis_size("ray") + lax.axis_index("ray")) * own_count
    zout, reqs = step(
        nz,
        ny,
        work_bricks,
        tile_slot.T,
        bricks,
        interp.transpose(1, 0, 2),
        weight_in,
        weight_mid,
        weight_out.T,
        spacing.T,
        targets,
    )
    return place(own_count, base.reshape(1), reqs, zout)


def solution(mesh):
    in_specs = (
        P(("group", "ray"), None),
        P("group", "ray"),
        P(("group", "ray"), None, None),
        P(("group", "ray"), None),
        P(("group", "ray"), None),
        P(None, ("group", "ray")),
        P(),
        P(),
        P(),
    )
    out_specs = P(("group", "ray"), None)
    return jax.shard_map(
        per_device, mesh=mesh, in_specs=in_specs, out_specs=out_specs, check_vma=False
    )
```

```python
import functools

import jax
import jax.numpy as jnp
from jax import lax
from jax.experimental import pallas as pl
from jax.experimental.pallas import tpu as pltpu
from jax.sharding import PartitionSpec as P

MESH = pl.DeviceIdType.MESH
F32 = jnp.float32
BF16 = jnp.bfloat16
NX = 4
NC = 2
PITCH = 40
SLICES = 4
HIGHEST = lax.Precision.HIGHEST


def coordinates():
    ray = lax.axis_index("ray")
    return ray // (NX * NC), (ray // NC) % NX, ray % NC


def ray_of(y, x, c):
    return (y * NX + x) * NC + c


class Peers:
    def __init__(self, nz, ny):
        self.nz, self.ny = nz, ny
        self.z = lax.axis_index("group")
        self.y, self.x, self.c = coordinates()

    def along_z(self, d):
        return {"group": lax.rem(self.z + d, self.nz)}

    def along_y(self, d):
        return {"ray": ray_of(lax.rem(self.y + d, self.ny), self.x, self.c)}

    def along_x(self, d):
        return {"ray": ray_of(self.y, lax.rem(self.x + d, NX), self.c)}

    def partner(self):
        return {"ray": ray_of(self.y, self.x, 1 - self.c)}

    def everybody(self):
        out = [self.along_z(d) for d in range(1, self.nz)]
        out += [self.along_y(d) for d in range(1, self.ny)]
        return out + [self.along_x(d) for d in range(1, NX)] + [self.partner()]

    def greet(self):
        sem = pltpu.get_barrier_semaphore()
        peers = self.everybody()
        for peer in peers:
            pl.semaphore_signal(sem, inc=1, device_id=peer, device_id_type=MESH)
        return lambda: pl.semaphore_wait(sem, len(peers))


class Copies:
    def __init__(self, send_sems, recv_sems):
        self.send_sems, self.recv_sems, self.count, self.live = send_sems, recv_sems, 0, []

    def make(self, src, dst, device):
        at = self.count
        self.count += 1
        copy = pltpu.make_async_remote_copy(
            src_ref=src,
            dst_ref=dst,
            send_sem=self.send_sems.at[at],
            recv_sem=self.recv_sems.at[at],
            device_id=device,
            device_id_type=MESH,
        )
        self.live.append(copy)
        return copy

    def start(self, src, dst, device):
        copy = self.make(src, dst, device)
        copy.start()
        return copy

    def drain(self):
        for copy in self.live:
            copy.wait_send()


def near_first(n):
    out = []
    for d in range(1, n // 2 + 1):
        out.append(d)
        if n - d != d:
            out.append(n - d)
    return out


def logistic(x):
    return 0.5 * jnp.tanh(0.5 * x) + 0.5


def silu_of_half(half):
    t = jnp.tanh(half)
    up = 1.0 + t
    act = half * up
    return act, up + act * (1.0 - t)


def iota(shape, axis):
    return lax.broadcasted_iota(jnp.int32, shape, axis)


def indicator(condition, dtype=F32):
    return jnp.where(condition, 1.0, 0.0).astype(dtype)


def step_copies(nz, ny):
    fetched = 2 * (nz - 1) + (nz - 1) + 2 * (ny - 1) + 3 * ny + 4 * ny
    return fetched + SLICES * (4 + 6 + (ny - 1) + (nz - 1))


def step_kernel(
    nz,
    ny,
    wb_ref,
    slots_ref,
    slotv_ref,
    bricks_hbm,
    interp_hbm,
    win_hbm,
    wmid_hbm,
    wout_hbm,
    spacing_hbm,
    targets_hbm,
    out_hbm,
    bricks_ref,
    interp_ref,
    win_ref,
    wmid_ref,
    wout_ref,
    spacing_ref,
    targets_ref,
    reqs_ref,
    out_ref,
    spread_s,
    zbuf,
    save_sems,
    mine,
    picks,
    sendb,
    arrived,
    gs,
    wc,
    feat_a,
    feat_b,
    slope_a,
    slope_b,
    raw_s,
    grad_s,
    order_s,
    parity_s,
    wsort,
    wturned,
    gnat,
    gsort,
    outb,
    part,
    cbuf,
    relay_a,
    relay_b,
    from_left,
    from_right,
    ybuf,
    load_sems,
    send_sems,
    recv_sems,
):
    peers = Peers(nz, ny)
    copies = Copies(send_sems, recv_sems)
    segs, rays, _ = interp_ref.shape
    tiles = segs * rays
    holders = NC * NX * ny
    cap = 2 * tiles // holders
    sorted_rows = holders * cap
    chunk = rays * 8
    steps = segs * 8
    pitch = rays + 8
    own_count = bricks_ref.shape[0]
    loads = []
    for n, (src, dst) in enumerate(
        (
            (interp_hbm, interp_ref),
            (bricks_hbm, bricks_ref),
            (win_hbm, win_ref),
            (wmid_hbm, wmid_ref),
            (wout_hbm, wout_ref),
            (spacing_hbm, spacing_ref),
            (targets_hbm, targets_ref),
        )
    ):
        loads.append(pltpu.make_async_copy(src, dst, load_sems.at[n]))
        loads[n].start()
    ask = jnp.where(iota(mine.shape, 0) == 0, wb_ref[0, 0], wb_ref[0, 1])
    mine[...] = ask
    reqs_ref[0] = ask
    barrier = peers.greet()

    slot = slotv_ref[...]
    holder = slot // 2
    rel_y = lax.rem(holder // (NX * NC) + (ny - peers.y), ny)
    rel_x = lax.rem(lax.rem(holder // NC, NX) + (NX - peers.x), NX)
    rel_c = jnp.abs(lax.rem(holder, NC) - peers.c)
    rel = ((rel_c * NX + rel_x) * ny + rel_y).astype(F32)
    parity = lax.rem(slot, 2).astype(F32)

    def as_row(x):
        return jnp.concatenate([x[seg : seg + 1] for seg in range(segs)], axis=1)

    rel, parity = as_row(rel), as_row(parity)
    named = rel == iota((holders, tiles), 0).astype(F32)
    before = indicator(iota((tiles, tiles), 0) < iota((tiles, tiles), 1), BF16)
    counts = jnp.dot(indicator(named, BF16), before, preferred_element_type=F32)
    rank = jnp.sum(jnp.where(named, counts, 0.0), axis=0, keepdims=True)
    taken = rel * cap + rank
    order_s[...] = indicator(iota((sorted_rows, tiles), 0).astype(F32) == taken, BF16)

    src, dst = iota((128, 512), 0), iota((128, 512), 1)
    voxel = src % 64
    perm = indicator(
        (dst // 128 == (src // 64) * 2 + voxel % 2) & (dst % 128 == voxel // 2), BF16
    )
    loads[0].wait()
    for seg in range(segs):
        for j in range(4):
            moved = jnp.dot(
                interp_ref[seg, :, j * 128 : (j + 1) * 128], perm, preferred_element_type=F32
            )
            for i2 in range(2):
                for h in range(2):
                    blk = i2 * 2 + h
                    wc[pl.ds(seg * rays * 24 + h * 8 + 2 * j + i2, rays, stride=24), :] = moved[
                        :, blk * 128 : (blk + 1) * 128
                    ]
    barrier()
    asks = [copies.start(mine, reqs_ref.at[nz - d], peers.along_z(d)) for d in near_first(nz)]

    natural = interp_ref[...].reshape(tiles, 512)
    ordered = jnp.dot(order_s[...], natural, preferred_element_type=F32)
    for j in range(4):
        pair = ordered[:, j * 128 : (j + 1) * 128]
        wsort[pl.ds(2 * j, sorted_rows, stride=8), :] = pair
        wsort[pl.ds(2 * j + 1, sorted_rows, stride=8), :] = pltpu.roll(pair, 64, 1)
    lane128 = iota((sorted_rows, 128), 1)
    wide = jnp.broadcast_to(parity, (128, tiles)).astype(BF16)
    odd = lax.dot_general(
        order_s[...], wide, (((1,), (1,)), ((), ())), preferred_element_type=F32
    )
    parity_s[...] = indicator((lane128 >= 64) == (odd > 0.5))

    def turn(first, last):
        for h in range(first, last):
            block = wsort[h * cap * 8 : (h + 1) * cap * 8, :]
            wturned[h] = jnp.transpose(block)[:64].astype(BF16)

    for load in loads[1:]:
        load.wait()
    for copy in asks:
        copy.wait_recv()
    base = (lax.axis_index("group") * lax.axis_size("ray") + lax.axis_index("ray")) * own_count
    rows = []
    for s in range(2):
        ids = jnp.concatenate([reqs_ref[e, s : s + 1, :] for e in range(nz)], axis=0)
        rows.append(indicator(ids - base == iota((nz, 128), 1)))
    choose = jnp.concatenate(rows, axis=0)
    spread_s[...] = jnp.transpose(choose)[:own_count]
    choose = choose[:, :own_count].astype(BF16)
    picked = jnp.dot(choose, bricks_ref[...], preferred_element_type=F32)
    gives = {}
    for s in range(2):
        for p in range(32):
            picks[pl.ds(s * nz * PITCH + p, nz, stride=PITCH), :] = picked[
                s * nz : (s + 1) * nz, p * 128 : (p + 1) * 128
            ]
        rows = picks[s * nz * PITCH : (s + 1) * nz * PITCH, :].reshape(nz, PITCH, 128)
        sendb[s] = rows[:, :32].astype(BF16)
        for d in near_first(nz):
            gives[s, d] = copies.start(sendb.at[s, d], arrived.at[s, nz - d], peers.along_z(d))
    turn(0, holders // 2)
    right, far, left = (peers.along_x(d) for d in (1, 2, 3))
    partner = peers.partner()
    order = [0] + [ny - d for d in near_first(ny)]
    spread, hops, cores = {}, {}, []

    def unit(c, j, e):
        y = lax.rem(peers.y + e, ny)
        x = lax.rem(peers.x + j, NX)
        return ray_of(y, x, c)

    def to_core(j, e):
        at = unit(peers.c, j, e)
        cores.append(copies.start(gs.at[at], gs.at[at], partner))

    def along_row(e):
        at = unit(peers.c, 0, e)
        for j, device in ((3, right), (1, left), (2, far)):
            hops[j, e] = copies.start(gs.at[at], gs.at[at], device)
        to_core(0, e)

    for s in range(2):
        held = sendb[s, 0].astype(F32)
        for d in near_first(nz):
            gives[s, d].wait_recv()
            held = held + arrived[s, nz - d].astype(F32)
        at = unit(peers.c, 0, 0)
        gs[at, s] = held.astype(BF16)
        for d in near_first(ny):
            spread[s, ny - d] = copies.start(gs.at[at, s], gs.at[at, s], peers.along_y(d))
    along_row(0)
    turn(holders // 2, holders)
    for e in order[1:]:
        spread[0, e].wait_recv()
        spread[1, e].wait_recv()
        along_row(e)
    for e in order:
        for j in (3, 1, 2):
            hops[j, e].wait_recv()
            to_core(j, e)
    for copy in cores:
        copy.wait_recv()

    win = win_ref[...] * 0.5
    wmid = wmid_ref[...] * 0.5
    wout = jnp.concatenate([wout_ref[...].astype(F32), jnp.zeros((4, 256), F32)], axis=0).astype(BF16)
    win_wide = jnp.concatenate([win.astype(F32), jnp.zeros((64, 256), F32)], axis=0).astype(BF16)

    def tiles_of(seg):
        for r in range(rays):
            name = slots_ref[seg, r]
            brick = gs[name >> 1, name & 1]
            at = (seg * rays + r) * 24
            weights = wc[at : at + 16, :][:, :32].astype(BF16)
            made = jnp.dot(weights, brick, preferred_element_type=F32)
            feat_a[seg % 2, pl.ds(r, 8, stride=pitch), :] = made[:8]
            feat_b[seg % 2, pl.ds(r, 8, stride=pitch), :] = made[8:]

    def forward(seg):
        rows = pl.ds(seg * chunk, chunk)
        features = feat_a[seg % 2] + pltpu.roll(feat_b[seg % 2], 64, 1)
        features = features.reshape(8, pitch, 128)[:, :rays].reshape(chunk, 128)
        features = features[:, :64].astype(BF16)
        act, slope_a[rows, :] = silu_of_half(jnp.dot(features, win, preferred_element_type=F32))
        act, slope_b[rows, :] = silu_of_half(
            jnp.dot(act.astype(BF16), wmid, preferred_element_type=F32)
        )
        raw = lax.dot_general(
            wout, act.astype(BF16), (((1,), (1,)), ((), ())), preferred_element_type=F32
        )
        turned = pltpu.roll(raw, chunk - rays, 1)
        for i in range(0, 8, 2):
            at = i * rays
            raw_s[pl.ds(seg * 8 + i, 8, stride=steps), :] = raw[:, at : at + 128]
            raw_s[pl.ds(seg * 8 + i + 1, 8, stride=steps), :] = turned[:, at : at + 128]

    tiles_of(0)
    for seg in range(segs):
        if seg + 1 < segs:
            tiles_of(seg + 1)
        forward(seg)

    spacing = spacing_ref[...]
    k0, k1 = iota((steps, steps), 0), iota((steps, steps), 1)
    earlier, later = indicator(k1 < k0), indicator(k1 > k0)
    raw0 = raw_s[0:steps, :][:, :rays]
    density = jnp.maximum(raw0, 0.0) + jnp.log1p(jnp.exp(-jnp.abs(raw0)))
    optical = density * spacing
    gone = jnp.dot(earlier, optical, precision=HIGHEST, preferred_element_type=F32)
    through = jnp.exp(-gone)
    kept = jnp.exp(-optical)
    weight = through * (1.0 - kept)
    pull = jnp.zeros_like(weight)
    grads = []
    for ch in range(3):
        shade = logistic(raw_s[(ch + 1) * steps : (ch + 2) * steps, :][:, :rays])
        colour = jnp.sum(weight * shade, axis=0, keepdims=True)
        err = colour - targets_ref[ch : ch + 1, :]
        pull = pull + err * shade
        grads.append(err * weight * shade * (1.0 - shade))
    after = jnp.dot(later, pull * weight, precision=HIGHEST, preferred_element_type=F32)
    grads.insert(0, (pull * through * kept - after) * spacing * logistic(raw0))
    grad_s[...] = jnp.zeros_like(grad_s)
    for ch in range(4):
        grad_s[ch * steps : (ch + 1) * steps, :rays] = grads[ch]

    for seg in range(segs):
        pieces = []
        for i in range(0, 8, 2):
            even = grad_s[pl.ds(seg * 8 + i, 8, stride=steps), :]
            uneven = grad_s[pl.ds(seg * 8 + i + 1, 8, stride=steps), :]
            pieces.append(even + pltpu.roll(uneven, rays, 1))
        raw_grad = jnp.concatenate(pieces, axis=1).astype(BF16)
        rows = pl.ds(seg * chunk, chunk)
        grad = lax.dot_general(
            raw_grad, wout, (((0,), (0,)), ((), ())), preferred_element_type=F32
        )
        slope = (grad * slope_b[rows, :]).astype(BF16)
        grad = lax.dot_general(slope, wmid, (((1,), (1,)), ((), ())), preferred_element_type=F32)
        slope = (grad * slope_a[rows, :]).astype(BF16)
        grad = lax.dot_general(
            slope, win_wide, (((1,), (1,)), ((), ())), preferred_element_type=F32
        )
        for j in range(4):
            even = grad[2 * j * rays : (2 * j + 1) * rays]
            uneven = grad[(2 * j + 1) * rays : (2 * j + 2) * rays]
            gnat[seg * rays : (seg + 1) * rays, j * 128 : (j + 1) * 128] = (
                even + pltpu.roll(uneven, 64, 1)
            ).astype(BF16)

    keep = parity_s[...]
    first = lane128 < 64
    for j in range(4):
        pair = jnp.dot(
            order_s[...], gnat[:, j * 128 : (j + 1) * 128], preferred_element_type=F32
        )
        swapped = pltpu.roll(pair, 64, 1)
        gsort[pl.ds(2 * j, sorted_rows, stride=8), :] = jnp.where(first, pair, swapped) * keep
        gsort[pl.ds(2 * j + 1, sorted_rows, stride=8), :] = jnp.where(first, swapped, pair) * keep

    def block(h):
        grads = gsort[h * cap * 8 : (h + 1) * cap * 8, :].astype(BF16)
        return jnp.dot(wturned[h], grads, preferred_element_type=F32)

    def cut(made, to, j, e):
        for q in range(SLICES):
            to[q, j, e] = made[q * depth : (q + 1) * depth]

    depth = 64 // SLICES
    half = ny // 2
    a, b = pl.ds(0, half), pl.ds(half, half)
    core, far_a, far_b, left_a, left_b, right_a, right_b = {}, {}, {}, {}, {}, {}, {}
    for j in (2, 1, 3, 0):
        for e in range(ny):
            cut(block((NX + j) * ny + e), outb, j, e)
        for q in range(SLICES):
            core[q, j] = copies.start(outb.at[q, j], cbuf.at[q, j], partner)
    for j in (2, 1, 3, 0):
        for e in range(ny):
            cut(block(j * ny + e), part, j, e)

    def merge(q, j):
        core[q, j].wait_recv()
        part[q, j] = part[q, j] + cbuf[q, j]

    def first_leg(q):
        merge(q, 2)
        far_a[q] = copies.start(part.at[q, 2, a], relay_a.at[q], right)
        far_b[q] = copies.start(part.at[q, 2, b], relay_b.at[q], left)
        merge(q, 1)
        left_b[q] = copies.start(part.at[q, 1, b], from_left.at[q, b], right)
        merge(q, 3)
        right_a[q] = copies.start(part.at[q, 3, a], from_right.at[q, a], left)

    def second_leg(q):
        far_a[q].wait_recv()
        part[q, 1, a] = part[q, 1, a] + relay_a[q]
        left_a[q] = copies.start(part.at[q, 1, a], from_left.at[q, a], right)
        far_b[q].wait_recv()
        part[q, 3, b] = part[q, 3, b] + relay_b[q]
        right_b[q] = copies.start(part.at[q, 3, b], from_right.at[q, b], left)
        merge(q, 0)

    ys, zs = {}, {}

    def along_columns(q):
        for copy in (right_a, left_a, left_b, right_b):
            copy[q].wait_recv()
        part[q, 0] = part[q, 0] + from_left[q] + from_right[q]
        for d in near_first(ny):
            ys[q, d] = copies.start(part.at[q, 0, d], ybuf.at[q, ny - d], peers.along_y(d))

    used = pl.ds(0, depth)

    def across_groups(q):
        total = part[q, 0, 0]
        for d in near_first(ny):
            ys[q, d].wait_recv()
            total = total + ybuf[q, ny - d]
        zbuf[q, 0, used] = total
        for d in near_first(nz):
            zs[q, d] = copies.start(
                zbuf.at[q, 0, used], zbuf.at[q, nz - d, used], peers.along_z(d)
            )

    saves = []
    left_side = iota((nz, 128), 1) < 64

    def land(q):
        for d in near_first(nz):
            zs[q, d].wait_recv()
        for v in range(0, depth, 2):
            even = jnp.concatenate([zbuf[q, e, v : v + 1] for e in range(nz)], axis=0)
            uneven = jnp.concatenate([zbuf[q, e, v + 1 : v + 2] for e in range(nz)], axis=0)
            rows = jnp.concatenate(
                [
                    jnp.where(left_side, even, pltpu.roll(uneven, 64, 1)),
                    jnp.where(left_side, pltpu.roll(even, 64, 1), uneven),
                ],
                axis=0,
            )
            at = (q * depth + v) * 64
            out_ref[:, at : at + 128] = jnp.dot(
                spread_s[...], rows, precision=HIGHEST, preferred_element_type=F32
            )
        lanes = pl.ds(q * depth * 64, depth * 64)
        saves.append(
            pltpu.make_async_copy(out_ref.at[:, lanes], out_hbm.at[:, lanes], save_sems.at[q])
        )
        saves[q].start()

    stages = (first_leg, second_leg, along_columns, across_groups, land)
    for stage in stages:
        for q in range(SLICES):
            stage(q)
    for save in saves:
        save.wait()
    copies.drain()


def step(nz, ny, work_bricks, slots, *operands):
    bricks, interp = operands[:2]
    segs, rays, _ = interp.shape
    tiles, samples, holders = segs * rays, segs * rays * 8, NC * NX * ny
    cap = 2 * tiles // holders
    total = step_copies(nz, ny)
    vmem = pl.BlockSpec(memory_space=pltpu.VMEM)
    smem = pl.BlockSpec(memory_space=pltpu.SMEM)
    hbm = pl.BlockSpec(memory_space=pltpu.HBM)
    unit = (32, 128)
    depth = 64 // SLICES
    every = pltpu.VMEM((SLICES, NX, ny, depth, 128), F32)
    whole = pltpu.VMEM((SLICES, ny, depth, 128), F32)
    half = pltpu.VMEM((SLICES, ny // 2, depth, 128), F32)
    return pl.pallas_call(
        functools.partial(step_kernel, nz, ny),
        out_shape=jax.ShapeDtypeStruct(bricks.shape, F32),
        in_specs=[smem, smem, vmem] + [hbm] * 7,
        out_specs=hbm,
        scratch_shapes=[
            pltpu.VMEM(x.shape, x.dtype)
            for x in (bricks, interp) + operands[2:]
        ]
        + [
            pltpu.VMEM((nz, 8, 128), jnp.int32),
            pltpu.VMEM(bricks.shape, F32),
            pltpu.VMEM((bricks.shape[0], 2 * nz), F32),
            pltpu.VMEM((SLICES, nz, depth + 8, 128), F32),
            pltpu.SemaphoreType.DMA((SLICES,)),
            pltpu.VMEM((8, 128), jnp.int32),
            pltpu.VMEM((2 * nz * PITCH, 128), F32),
            pltpu.VMEM((2, nz) + unit, BF16),
            pltpu.VMEM((2, nz) + unit, BF16),
            pltpu.VMEM((holders, 2) + unit, BF16),
            pltpu.VMEM((tiles * 24, 128), F32),
            pltpu.VMEM((2, (rays + 8) * 8, 128), F32),
            pltpu.VMEM((2, (rays + 8) * 8, 128), F32),
            pltpu.VMEM((samples, 256), F32),
            pltpu.VMEM((samples, 256), F32),
            pltpu.VMEM((8 * segs * 8, 128), F32),
            pltpu.VMEM((8 * segs * 8, 128), F32),
            pltpu.VMEM((holders * cap, tiles), BF16),
            pltpu.VMEM((holders * cap, 128), F32),
            pltpu.VMEM((holders * cap * 8, 128), F32),
            pltpu.VMEM((holders, 64, cap * 8), BF16),
            pltpu.VMEM((tiles, 512), BF16),
            pltpu.VMEM((holders * cap * 8, 128), F32),
            every,
            every,
            every,
            half,
            half,
            whole,
            whole,
            whole,
            pltpu.SemaphoreType.DMA((7,)),
            pltpu.SemaphoreType.DMA((total,)),
            pltpu.SemaphoreType.DMA((total,)),
        ],
        compiler_params=pltpu.CompilerParams(collective_id=0, has_side_effects=True),
        name="step",
    )(work_bricks, slots, slots, *operands)


def per_device(
    bricks, work_bricks, interp, tile_slot, spacing, targets, weight_in, weight_mid, weight_out
):
    nz = lax.axis_size("group")
    ny = lax.axis_size("ray") // (NX * NC)
    return step(
        nz,
        ny,
        work_bricks,
        tile_slot.T,
        bricks,
        interp.transpose(1, 0, 2),
        weight_in,
        weight_mid,
        weight_out.T,
        spacing.T,
        targets,
    )


def solution(mesh):
    in_specs = (
        P(("group", "ray"), None),
        P("group", "ray"),
        P(("group", "ray"), None, None),
        P(("group", "ray"), None),
        P(("group", "ray"), None),
        P(None, ("group", "ray")),
        P(),
        P(),
        P(),
    )
    out_specs = P(("group", "ray"), None)
    return jax.shard_map(
        per_device, mesh=mesh, in_specs=in_specs, out_specs=out_specs, check_vma=False
    )
```

```python
import functools

import jax
import jax.numpy as jnp
from jax import lax
from jax.experimental import pallas as pl
from jax.experimental.pallas import tpu as pltpu
from jax.sharding import PartitionSpec as P

MESH = pl.DeviceIdType.MESH
F32 = jnp.float32
BF16 = jnp.bfloat16
NX = 4
NC = 2
PITCH = 40
SLICES = 4
HIGHEST = lax.Precision.HIGHEST


def coordinates():
    ray = lax.axis_index("ray")
    return ray // (NX * NC), (ray // NC) % NX, ray % NC


def ray_of(y, x, c):
    return (y * NX + x) * NC + c


class Peers:
    def __init__(self, nz, ny):
        self.nz, self.ny = nz, ny
        self.z = lax.axis_index("group")
        self.y, self.x, self.c = coordinates()

    def along_z(self, d):
        return {"group": lax.rem(self.z + d, self.nz)}

    def along_y(self, d):
        return {"ray": ray_of(lax.rem(self.y + d, self.ny), self.x, self.c)}

    def along_x(self, d):
        return {"ray": ray_of(self.y, lax.rem(self.x + d, NX), self.c)}

    def partner(self):
        return {"ray": ray_of(self.y, self.x, 1 - self.c)}

    def everybody(self):
        out = [self.along_z(d) for d in far_first(self.nz)]
        out += [self.along_y(d) for d in far_first(self.ny)]
        return out + [self.along_x(d) for d in range(1, NX)] + [self.partner()]

    def greet(self):
        sem = pltpu.get_barrier_semaphore()
        peers = self.everybody()
        for peer in peers:
            pl.semaphore_signal(sem, inc=1, device_id=peer, device_id_type=MESH)
        return lambda: pl.semaphore_wait(sem, len(peers))


class Copies:
    def __init__(self, send_sems, recv_sems):
        self.send_sems, self.recv_sems, self.count, self.live = send_sems, recv_sems, 0, []

    def make(self, src, dst, device):
        at = self.count
        self.count += 1
        copy = pltpu.make_async_remote_copy(
            src_ref=src,
            dst_ref=dst,
            send_sem=self.send_sems.at[at],
            recv_sem=self.recv_sems.at[at],
            device_id=device,
            device_id_type=MESH,
        )
        self.live.append(copy)
        return copy

    def start(self, src, dst, device):
        copy = self.make(src, dst, device)
        copy.start()
        return copy

    def drain(self):
        for copy in self.live:
            copy.wait_send()
        self.live = []


def far_first(n):
    return sorted(range(1, n), key=lambda d: -min(d, n - d))


def near_first(n):
    return far_first(n)[::-1]


def logistic(x):
    return 0.5 * jnp.tanh(0.5 * x) + 0.5


def silu_of_half(half):
    t = jnp.tanh(half)
    up = 1.0 + t
    act = half * up
    return act, up + act * (1.0 - t)


def iota(shape, axis):
    return lax.broadcasted_iota(jnp.int32, shape, axis)


def indicator(condition, dtype=F32):
    return jnp.where(condition, 1.0, 0.0).astype(dtype)


def step_copies(nz, ny):
    fetched = 2 * (nz - 1) + (nz - 1) + 2 * (ny - 1) + 3 * ny + 4 * ny
    return fetched + SLICES * (4 + 6 + (ny - 1) + (nz - 1)) - 3


def step_kernel(
    nz,
    ny,
    wb_hbm,
    slots_hbm,
    bricks_hbm,
    interp_hbm,
    win_hbm,
    wmid_hbm,
    wout_hbm,
    spacing_hbm,
    targets_hbm,
    out_hbm,
    bricks_ref,
    interp_ref,
    win_ref,
    wmid_ref,
    wout_ref,
    spacing_ref,
    targets_ref,
    wb_ref,
    slots_ref,
    slotv_ref,
    reqs_ref,
    out_ref,
    spread_s,
    zbuf,
    save_sems,
    mine,
    picks,
    sendb,
    arrived,
    gs,
    wc,
    feat_a,
    feat_b,
    slope_a,
    slope_b,
    raw_s,
    grad_s,
    order_s,
    parity_s,
    wsort,
    wturned,
    gnat,
    gsort,
    outb,
    part,
    cbuf,
    relay_a,
    relay_b,
    from_left,
    from_right,
    ybuf,
    columns,
    across,
    load_sems,
    send_sems,
    recv_sems,
):
    peers = Peers(nz, ny)
    copies = Copies(send_sems, recv_sems)
    segs, rays, _ = interp_ref.shape
    tiles = segs * rays
    holders = NC * NX * ny
    cap = 2 * tiles // holders
    sorted_rows = holders * cap
    chunk = rays * 8
    steps = segs * 8
    pitch = rays + 8
    own_count = bricks_ref.shape[0]
    barrier = peers.greet()
    loads = []
    for n, (src, dst) in enumerate(
        (
            (wb_hbm, wb_ref),
            (slots_hbm, slotv_ref),
            (interp_hbm, interp_ref),
            (slots_hbm, slots_ref),
            (bricks_hbm, bricks_ref),
            (win_hbm, win_ref),
            (wmid_hbm, wmid_ref),
            (wout_hbm, wout_ref),
            (spacing_hbm, spacing_ref),
            (targets_hbm, targets_ref),
        )
    ):
        loads.append(pltpu.make_async_copy(src, dst, load_sems.at[n]))
        loads[n].start()
    loads[0].wait()
    ask = jnp.where(iota(mine.shape, 0) == 0, wb_ref[0, 0], wb_ref[0, 1])
    mine[...] = ask
    reqs_ref[0] = ask
    loads[1].wait()

    slot = slotv_ref[...]
    holder = slot // 2
    rel_y = lax.rem(holder // (NX * NC) + (ny - peers.y), ny)
    rel_x = lax.rem(lax.rem(holder // NC, NX) + (NX - peers.x), NX)
    rel_c = jnp.abs(lax.rem(holder, NC) - peers.c)
    rel = ((rel_c * NX + rel_x) * ny + rel_y).astype(F32)
    parity = lax.rem(slot, 2).astype(F32)

    def as_row(x):
        return jnp.concatenate([x[seg : seg + 1] for seg in range(segs)], axis=1)

    rel, parity = as_row(rel), as_row(parity)
    named = rel == iota((holders, tiles), 0).astype(F32)
    before = indicator(iota((tiles, tiles), 0) < iota((tiles, tiles), 1), BF16)
    counts = jnp.dot(indicator(named, BF16), before, preferred_element_type=F32)
    rank = jnp.sum(jnp.where(named, counts, 0.0), axis=0, keepdims=True)
    taken = rel * cap + rank
    order_s[...] = indicator(iota((sorted_rows, tiles), 0).astype(F32) == taken, BF16)

    src, dst = iota((128, 512), 0), iota((128, 512), 1)
    voxel = src % 64
    perm = indicator(
        (dst // 128 == (src // 64) * 2 + voxel % 2) & (dst % 128 == voxel // 2), BF16
    )
    loads[2].wait()
    for seg in range(segs):
        for j in range(4):
            moved = jnp.dot(
                interp_ref[seg, :, j * 128 : (j + 1) * 128], perm, preferred_element_type=F32
            )
            for i2 in range(2):
                for h in range(2):
                    blk = i2 * 2 + h
                    wc[pl.ds(seg * rays * 24 + h * 8 + 2 * j + i2, rays, stride=24), :] = moved[
                        :, blk * 128 : (blk + 1) * 128
                    ]
    barrier()
    asks = [copies.start(mine, reqs_ref.at[nz - d], peers.along_z(d)) for d in far_first(nz)]

    natural = interp_ref[...].reshape(tiles, 512)
    ordered = jnp.dot(order_s[...], natural, preferred_element_type=F32)
    for j in range(4):
        pair = ordered[:, j * 128 : (j + 1) * 128]
        wsort[pl.ds(2 * j, sorted_rows, stride=8), :] = pair
        wsort[pl.ds(2 * j + 1, sorted_rows, stride=8), :] = pltpu.roll(pair, 64, 1)
    lane128 = iota((sorted_rows, 128), 1)
    wide = jnp.broadcast_to(parity, (128, tiles)).astype(BF16)
    odd = lax.dot_general(
        order_s[...], wide, (((1,), (1,)), ((), ())), preferred_element_type=F32
    )
    parity_s[...] = indicator((lane128 >= 64) == (odd > 0.5))

    def turn(first, last):
        for h in range(first, last):
            block = wsort[h * cap * 8 : (h + 1) * cap * 8, :]
            wturned[h] = jnp.transpose(block)[:64].astype(BF16)

    for load in loads[3:]:
        load.wait()
    for copy in asks:
        copy.wait_recv()
    base = (lax.axis_index("group") * lax.axis_size("ray") + lax.axis_index("ray")) * own_count
    rows = []
    for s in range(2):
        ids = jnp.concatenate([reqs_ref[e, s : s + 1, :] for e in range(nz)], axis=0)
        rows.append(indicator(ids - base == iota((nz, 128), 1)))
    choose = jnp.concatenate(rows, axis=0)
    spread_s[...] = jnp.transpose(choose)[:own_count]
    choose = choose[:, :own_count].astype(BF16)
    picked = jnp.dot(choose, bricks_ref[...], preferred_element_type=F32)
    gives = {}
    for s in range(2):
        for p in range(32):
            picks[pl.ds(s * nz * PITCH + p, nz, stride=PITCH), :] = picked[
                s * nz : (s + 1) * nz, p * 128 : (p + 1) * 128
            ]
        rows = picks[s * nz * PITCH : (s + 1) * nz * PITCH, :].reshape(nz, PITCH, 128)
        sendb[s] = rows[:, :32].astype(BF16)
        for d in far_first(nz):
            gives[s, d] = copies.start(sendb.at[s, d], arrived.at[s, nz - d], peers.along_z(d))
    turn(0, holders // 2)
    right, far, left = (peers.along_x(d) for d in (1, 2, 3))
    partner = peers.partner()
    order = [0] + [ny - d for d in near_first(ny)]
    spread, hops, cores = {}, {}, []

    def unit(c, j, e):
        y = lax.rem(peers.y + e, ny)
        x = lax.rem(peers.x + j, NX)
        return ray_of(y, x, c)

    def to_core(j, e):
        at = unit(peers.c, j, e)
        cores.append(copies.start(gs.at[at], gs.at[at], partner))

    def along_row(e):
        at = unit(peers.c, 0, e)
        for j, device in ((2, far), (3, right), (1, left)):
            hops[j, e] = copies.start(gs.at[at], gs.at[at], device)
        to_core(0, e)

    for s in range(2):
        held = sendb[s, 0].astype(F32)
        for d in near_first(nz):
            gives[s, d].wait_recv()
            held = held + arrived[s, nz - d].astype(F32)
        at = unit(peers.c, 0, 0)
        gs[at, s] = held.astype(BF16)
        for d in far_first(ny):
            spread[s, ny - d] = copies.start(gs.at[at, s], gs.at[at, s], peers.along_y(d))
    along_row(0)
    turn(holders // 2, holders)
    for e in order[1:]:
        spread[0, e].wait_recv()
        spread[1, e].wait_recv()
        along_row(e)
    for e in order:
        for j in (3, 1, 2):
            hops[j, e].wait_recv()
            to_core(j, e)
    for copy in cores:
        copy.wait_recv()

    win = win_ref[...] * 0.5
    wmid = wmid_ref[...] * 0.5
    wout = jnp.concatenate([wout_ref[...].astype(F32), jnp.zeros((4, 256), F32)], axis=0).astype(BF16)
    win_wide = jnp.concatenate([win.astype(F32), jnp.zeros((64, 256), F32)], axis=0).astype(BF16)

    def tiles_of(seg):
        for r in range(rays):
            name = slots_ref[seg, r]
            brick = gs[name >> 1, name & 1]
            at = (seg * rays + r) * 24
            weights = wc[at : at + 16, :][:, :32].astype(BF16)
            made = jnp.dot(weights, brick, preferred_element_type=F32)
            feat_a[seg % 2, pl.ds(r, 8, stride=pitch), :] = made[:8]
            feat_b[seg % 2, pl.ds(r, 8, stride=pitch), :] = made[8:]

    def forward(seg):
        rows = pl.ds(seg * chunk, chunk)
        features = feat_a[seg % 2] + pltpu.roll(feat_b[seg % 2], 64, 1)
        features = features.reshape(8, pitch, 128)[:, :rays].reshape(chunk, 128)
        features = features[:, :64].astype(BF16)
        act, slope_a[rows, :] = silu_of_half(jnp.dot(features, win, preferred_element_type=F32))
        act, slope_b[rows, :] = silu_of_half(
            jnp.dot(act.astype(BF16), wmid, preferred_element_type=F32)
        )
        raw = lax.dot_general(
            wout, act.astype(BF16), (((1,), (1,)), ((), ())), preferred_element_type=F32
        )
        turned = pltpu.roll(raw, chunk - rays, 1)
        for i in range(0, 8, 2):
            at = i * rays
            raw_s[pl.ds(seg * 8 + i, 8, stride=steps), :] = raw[:, at : at + 128]
            raw_s[pl.ds(seg * 8 + i + 1, 8, stride=steps), :] = turned[:, at : at + 128]

    tiles_of(0)
    for seg in range(segs):
        if seg + 1 < segs:
            tiles_of(seg + 1)
        forward(seg)

    spacing = spacing_ref[...]
    k0, k1 = iota((steps, steps), 0), iota((steps, steps), 1)
    earlier, later = indicator(k1 < k0), indicator(k1 > k0)
    raw0 = raw_s[0:steps, :][:, :rays]
    density = jnp.maximum(raw0, 0.0) + jnp.log1p(jnp.exp(-jnp.abs(raw0)))
    optical = density * spacing
    gone = jnp.dot(earlier, optical, precision=HIGHEST, preferred_element_type=F32)
    through = jnp.exp(-gone)
    kept = jnp.exp(-optical)
    weight = through * (1.0 - kept)
    pull = jnp.zeros_like(weight)
    grads = []
    for ch in range(3):
        shade = logistic(raw_s[(ch + 1) * steps : (ch + 2) * steps, :][:, :rays])
        colour = jnp.sum(weight * shade, axis=0, keepdims=True)
        err = colour - targets_ref[ch : ch + 1, :]
        pull = pull + err * shade
        grads.append(err * weight * shade * (1.0 - shade))
    after = jnp.dot(later, pull * weight, precision=HIGHEST, preferred_element_type=F32)
    grads.insert(0, (pull * through * kept - after) * spacing * logistic(raw0))
    grad_s[...] = jnp.zeros_like(grad_s)
    for ch in range(4):
        grad_s[ch * steps : (ch + 1) * steps, :rays] = grads[ch]

    for seg in range(segs):
        pieces = []
        for i in range(0, 8, 2):
            even = grad_s[pl.ds(seg * 8 + i, 8, stride=steps), :]
            uneven = grad_s[pl.ds(seg * 8 + i + 1, 8, stride=steps), :]
            pieces.append(even + pltpu.roll(uneven, rays, 1))
        raw_grad = jnp.concatenate(pieces, axis=1).astype(BF16)
        rows = pl.ds(seg * chunk, chunk)
        grad = lax.dot_general(
            raw_grad, wout, (((0,), (0,)), ((), ())), preferred_element_type=F32
        )
        slope = (grad * slope_b[rows, :]).astype(BF16)
        grad = lax.dot_general(slope, wmid, (((1,), (1,)), ((), ())), preferred_element_type=F32)
        slope = (grad * slope_a[rows, :]).astype(BF16)
        grad = lax.dot_general(
            slope, win_wide, (((1,), (1,)), ((), ())), preferred_element_type=F32
        )
        for j in range(4):
            even = grad[2 * j * rays : (2 * j + 1) * rays]
            uneven = grad[(2 * j + 1) * rays : (2 * j + 2) * rays]
            gnat[seg * rays : (seg + 1) * rays, j * 128 : (j + 1) * 128] = (
                even + pltpu.roll(uneven, 64, 1)
            ).astype(BF16)

    keep = parity_s[...]
    first = lane128 < 64
    for j in range(4):
        pair = jnp.dot(
            order_s[...], gnat[:, j * 128 : (j + 1) * 128], preferred_element_type=F32
        )
        swapped = pltpu.roll(pair, 64, 1)
        gsort[pl.ds(2 * j, sorted_rows, stride=8), :] = jnp.where(first, pair, swapped) * keep
        gsort[pl.ds(2 * j + 1, sorted_rows, stride=8), :] = jnp.where(first, swapped, pair) * keep

    def block(h):
        grads = gsort[h * cap * 8 : (h + 1) * cap * 8, :].astype(BF16)
        return jnp.dot(wturned[h], grads, preferred_element_type=F32)

    def cut(made, to, j, e):
        for q in range(SLICES):
            to[q, j, e] = made[q * depth : (q + 1) * depth]

    depth = 64 // SLICES
    half = ny // 2
    a, b = pl.ds(0, half), pl.ds(half, half)
    core, far_a, far_b, left_a, left_b, right_a, right_b = {}, {}, {}, {}, {}, {}, {}
    for j in (2, 1, 3, 0):
        for e in range(ny):
            cut(block((NX + j) * ny + e), outb, j, e)
        for q in range(SLICES):
            core[q, j] = copies.start(outb.at[q, j], cbuf.at[q, j], partner)
    for j in (2, 1, 3, 0):
        for e in range(ny):
            cut(block(j * ny + e), part, j, e)

    def merge(q, j):
        core[q, j].wait_recv()
        part[q, j] = part[q, j] + cbuf[q, j]

    def first_leg(q):
        merge(q, 2)
        far_a[q] = copies.start(part.at[q, 2, a], relay_a.at[q], right)
        far_b[q] = copies.start(part.at[q, 2, b], relay_b.at[q], left)
        merge(q, 1)
        left_b[q] = copies.start(part.at[q, 1, b], from_left.at[q, b], right)
        merge(q, 3)
        right_a[q] = copies.start(part.at[q, 3, a], from_right.at[q, a], left)

    def second_leg(q):
        far_a[q].wait_recv()
        part[q, 1, a] = part[q, 1, a] + relay_a[q]
        left_a[q] = copies.start(part.at[q, 1, a], from_left.at[q, a], right)
        far_b[q].wait_recv()
        part[q, 3, b] = part[q, 3, b] + relay_b[q]
        right_b[q] = copies.start(part.at[q, 3, b], from_right.at[q, b], left)
        merge(q, 0)

    xs, ys, zs = {}, {}, {}

    def along_columns(q):
        for copy in (right_a, left_a, left_b, right_b):
            copy[q].wait_recv()
        part[q, 0] = part[q, 0] + from_left[q] + from_right[q]
        for d in far_first(ny):
            ys[q, d] = copies.start(part.at[q, 0, d], ybuf.at[q, ny - d], peers.along_y(d))

    used = pl.ds(0, depth)

    last = SLICES - 1

    def columns_first():
        for j in (2, 1, 3, 0):
            merge(last, j)
        for d in far_first(ny):
            ys[last, d] = copies.start(
                part.at[last, :, d], columns.at[ny - d], peers.along_y(d)
            )

    def rows_second():
        for d in near_first(ny):
            ys[last, d].wait_recv()
            part[last, :, 0] = part[last, :, 0] + columns[ny - d]
        for j in (2, 1, 3):
            xs[j] = copies.start(part.at[last, j, 0], across.at[NX - j], peers.along_x(j))

    def across_groups(q):
        total = part[q, 0, 0]
        if q == last:
            for j in (1, 3, 2):
                xs[j].wait_recv()
                total = total + across[NX - j]
        else:
            for d in near_first(ny):
                ys[q, d].wait_recv()
                total = total + ybuf[q, ny - d]
        zbuf[q, 0, used] = total
        for d in far_first(nz):
            zs[q, d] = copies.start(
                zbuf.at[q, 0, used], zbuf.at[q, nz - d, used], peers.along_z(d)
            )

    saves = []
    left_side = iota((nz, 128), 1) < 64

    def land(q):
        for d in near_first(nz):
            zs[q, d].wait_recv()
        for v in range(0, depth, 2):
            even = jnp.concatenate([zbuf[q, e, v : v + 1] for e in range(nz)], axis=0)
            uneven = jnp.concatenate([zbuf[q, e, v + 1 : v + 2] for e in range(nz)], axis=0)
            rows = jnp.concatenate(
                [
                    jnp.where(left_side, even, pltpu.roll(uneven, 64, 1)),
                    jnp.where(left_side, pltpu.roll(even, 64, 1), uneven),
                ],
                axis=0,
            )
            at = (q * depth + v) * 64
            out_ref[:, at : at + 128] = jnp.dot(
                spread_s[...], rows, precision=HIGHEST, preferred_element_type=F32
            )
        lanes = pl.ds(q * depth * 64, depth * 64)
        saves.append(
            pltpu.make_async_copy(out_ref.at[:, lanes], out_hbm.at[:, lanes], save_sems.at[q])
        )
        saves[q].start()

    sent, copies.live = copies.live, []
    first_leg(0)
    columns_first()
    for q in range(1, last):
        first_leg(q)
    for copy in sent:
        copy.wait_send()
    for q in range(last):
        second_leg(q)
    for q in range(last - 1):
        along_columns(q)
    rows_second()
    along_columns(last - 1)
    sent, copies.live = copies.live, []
    for q in range(last):
        across_groups(q)
    for copy in sent:
        copy.wait_send()
    across_groups(last)
    for q in range(SLICES):
        land(q)
    for save in saves:
        save.wait()
    copies.drain()


def step(nz, ny, work_bricks, slots, *operands):
    bricks, interp = operands[:2]
    segs, rays, _ = interp.shape
    tiles, samples, holders = segs * rays, segs * rays * 8, NC * NX * ny
    cap = 2 * tiles // holders
    total = step_copies(nz, ny)
    hbm = pl.BlockSpec(memory_space=pltpu.HBM)
    unit = (32, 128)
    depth = 64 // SLICES
    every = pltpu.VMEM((SLICES, NX, ny, depth, 128), F32)
    whole = pltpu.VMEM((SLICES, ny, depth, 128), F32)
    half = pltpu.VMEM((SLICES, ny // 2, depth, 128), F32)
    return pl.pallas_call(
        functools.partial(step_kernel, nz, ny),
        out_shape=jax.ShapeDtypeStruct(bricks.shape, F32),
        in_specs=[hbm] * 9,
        out_specs=hbm,
        scratch_shapes=[
            pltpu.VMEM(x.shape, x.dtype)
            for x in (bricks, interp) + operands[2:]
        ]
        + [
            pltpu.SMEM(work_bricks.shape, jnp.int32),
            pltpu.SMEM(slots.shape, jnp.int32),
            pltpu.VMEM(slots.shape, jnp.int32),
            pltpu.VMEM((nz, 8, 128), jnp.int32),
            pltpu.VMEM(bricks.shape, F32),
            pltpu.VMEM((bricks.shape[0], 2 * nz), F32),
            pltpu.VMEM((SLICES, nz, depth + 8, 128), F32),
            pltpu.SemaphoreType.DMA((SLICES,)),
            pltpu.VMEM((8, 128), jnp.int32),
            pltpu.VMEM((2 * nz * PITCH, 128), F32),
            pltpu.VMEM((2, nz) + unit, BF16),
            pltpu.VMEM((2, nz) + unit, BF16),
            pltpu.VMEM((holders, 2) + unit, BF16),
            pltpu.VMEM((tiles * 24, 128), F32),
            pltpu.VMEM((2, (rays + 8) * 8, 128), F32),
            pltpu.VMEM((2, (rays + 8) * 8, 128), F32),
            pltpu.VMEM((samples, 256), F32),
            pltpu.VMEM((samples, 256), F32),
            pltpu.VMEM((8 * segs * 8, 128), F32),
            pltpu.VMEM((8 * segs * 8, 128), F32),
            pltpu.VMEM((holders * cap, tiles), BF16),
            pltpu.VMEM((holders * cap, 128), F32),
            pltpu.VMEM((holders * cap * 8, 128), F32),
            pltpu.VMEM((holders, 64, cap * 8), BF16),
            pltpu.VMEM((tiles, 512), BF16),
            pltpu.VMEM((holders * cap * 8, 128), F32),
            every,
            every,
            every,
            half,
            half,
            whole,
            whole,
            whole,
            pltpu.VMEM((ny, NX, depth, 128), F32),
            pltpu.VMEM((NX, depth, 128), F32),
            pltpu.SemaphoreType.DMA((10,)),
            pltpu.SemaphoreType.DMA((total,)),
            pltpu.SemaphoreType.DMA((total,)),
        ],
        compiler_params=pltpu.CompilerParams(collective_id=0, has_side_effects=True),
        name="step",
    )(work_bricks, slots, *operands)


def per_device(
    bricks, work_bricks, interp, tile_slot, spacing, targets, weight_in, weight_mid, weight_out
):
    nz = lax.axis_size("group")
    ny = lax.axis_size("ray") // (NX * NC)
    return step(
        nz,
        ny,
        work_bricks,
        tile_slot.T,
        bricks,
        interp.transpose(1, 0, 2),
        weight_in,
        weight_mid,
        weight_out.T,
        spacing.T,
        targets,
    )


def solution(mesh):
    in_specs = (
        P(("group", "ray"), None),
        P("group", "ray"),
        P(("group", "ray"), None, None),
        P(("group", "ray"), None),
        P(("group", "ray"), None),
        P(None, ("group", "ray")),
        P(),
        P(),
        P(),
    )
    out_specs = P(("group", "ray"), None)
    return jax.shard_map(
        per_device, mesh=mesh, in_specs=in_specs, out_specs=out_specs, check_vma=False
    )
```
